32 devices in a mesh: dom: 8 (over z, y), tm: 4 (over x, core).
Axes of the slice: x: 2, y: 2, z: 4, core: 2. Of those that a mesh axis runs over, the one named last changes fastest.
Arguments:
- panel_signal: bfloat16 [8, 8192], P('tm', 'dom'), may hold values from -6 to 6
- panel_box: int32 [8192], P('dom'), may hold values from 0 to 15
- radiation: bfloat16 [8192, 1024], P('dom'), may hold values from -0.75 to 0.75
- reception: bfloat16 [8192, 1024], P('dom'), may hold values from -0.1875 to 0.1875
- translation: bfloat16 [64, 8, 1024], P(None, None, 'dom'), may hold values from -1 to 1
- list_source: int32 [128, 8], replicated, may hold values from 0 to 127
- list_class: int32 [128, 8], replicated, may hold values from 0 to 63
- list_count: int32 [128], replicated, may hold values from 1 to 8, as said below
Outputs:
- panel_field: bfloat16 [8, 8192], P('tm', 'dom')
The draws below stay inside these ranges and needn't reach their ends.
Inputs may be any that keep to these rules, and one draw needn't show every extreme that they name: `panel_box`: indices a panel's box among the 16 boxes of its own index of dom. Box a uses the first list_count[a] entries of its lists; the rest are padding.
All inputs are finite; a program needn't handle non-finite values.
Results may differ from the reference program's by a relative error of at most 0.0057.
Values may be sent and summed in bfloat16 or wider, within the bound.
A program may use at most 64 MiB of HBM per device.

```python
import math
import jax
import jax.numpy as jnp
import numpy as np
from jax import lax

K = 1024
PAN_DEV = 1024
BOX_DEV = 16
J = 8
C = 64
TS = 8
B = 128
PAN = 8192
N_DOM = 8


def draw_list_count(key, part):
    counts = jax.random.randint(jax.random.fold_in(key, 7), (B,), 1, J + 1)
    return counts.at[0].set(J).astype(jnp.int32)


def with_ends(values, key, low, largest):
    spot = [jax.random.randint(jax.random.fold_in(key, axis), (), 0, length) for axis, length in enumerate(values.shape)]
    widest = values.shape.index(max(values.shape))
    next_to = spot[:widest] + [(spot[widest] + 1) % values.shape[widest]] + spot[widest + 1:]
    return values.at[tuple(spot)].set(low).at[tuple(next_to)].set(largest)


def levels(rng, shape, cuts, least, largest):
    def one(dim, parts):
        steps = jax.random.uniform(jax.random.fold_in(jax.random.fold_in(rng, 6), dim), (parts,), jnp.float32, least / len(cuts), largest / len(cuts))
        return jnp.repeat(jnp.exp(steps), shape[dim] // parts).reshape((-1,) + (1,) * (len(shape) - dim - 1))

    factor_of = one(*cuts[0])
    for cut in cuts[1:]:
        factor_of = factor_of * one(*cut)
    return factor_of


def rank_table(number_of, skew):
    portions = [(1 << 20) // math.isqrt(standing ** skew) + 1 for standing in range(1, number_of + 1)]
    spread = 1 + sum(portions) // (1 << 30)
    return np.cumsum(np.array([max(1, weight // spread) for weight in portions]))


def ranked(own_key, extent, count, lean):
    table = rank_table(count, lean)
    pick = jax.random.randint(jax.random.fold_in(own_key, 1), extent, 0, int(table[count - 1]))
    grade = jnp.searchsorted(jnp.asarray(table, jnp.int32), pick, side="right")
    return jax.random.permutation(jax.random.fold_in(own_key, 2), count)[grade].astype(jnp.int32)


def gaussian(key, dims, scale, limit, shards=(), kind=jnp.bfloat16):
    drawn = jax.random.normal(key, dims, jnp.float32) * scale
    if len(shards) > 0:
        drawn = levels(key, dims, shards, -0.22, 0.18) * drawn
    return jnp.clip(drawn, min=-limit, max=limit).astype(kind)


def setup_inputs(seed: int = 0) -> dict:
    key_of = jax.random.split(jax.random.key(seed), 9)
    panel_signal = gaussian(key_of[0], (TS, PAN), 1.0, 6.0, ((0, 4), (1, 8)))
    panel_box = with_ends(ranked(key_of[1], (PAN,), BOX_DEV, 2), jax.random.fold_in(key_of[1], 3), 0, BOX_DEV - 1).astype(jnp.int32)
    radiation = gaussian(key_of[2], (PAN, K), (PAN_DEV // BOX_DEV) ** -0.5, 0.75, ((0, 8),))
    reception = gaussian(key_of[3], (PAN, K), K ** -0.5, 0.1875, ((0, 8),))
    translation = gaussian(key_of[4], (C, TS, K), (J * TS // 2) ** -0.5, 1.0, ((2, 8),))
    list_source = with_ends(jax.random.randint(key_of[5], (B, J), 0, B), jax.random.fold_in(key_of[5], 1), 0, B - 1).astype(jnp.int32)
    list_class = with_ends(jax.random.randint(key_of[6], (B, J), 0, C), jax.random.fold_in(key_of[6], 1), 0, C - 1).astype(jnp.int32)
    list_count = draw_list_count(jax.random.fold_in(key_of[8], 71), 0)
    return {"panel_signal": panel_signal, "panel_box": panel_box, "radiation": radiation, "reception": reception, "translation": translation, "list_source": list_source, "list_class": list_class, "list_count": list_count}


def aggregate_block(signal, owner, weights):
    count_rows = signal.shape[0]
    box_onehot = (owner[None, :] == jnp.arange(BOX_DEV, dtype=jnp.int32)[:, None]).astype(signal.dtype)
    masked = (signal[:, None, :] * box_onehot[None]).reshape(count_rows * BOX_DEV, PAN_DEV)
    summed = jnp.dot(masked, weights, preferred_element_type=jnp.float32)
    return summed.astype(jnp.bfloat16).reshape(count_rows, BOX_DEV, K)


def reference(panel_signal, panel_box, radiation, reception, translation, list_source, list_class, list_count):
    def outgoing_block(index):
        signal = lax.dynamic_slice_in_dim(panel_signal, index * PAN_DEV, PAN_DEV, 1)
        owner = lax.dynamic_slice_in_dim(panel_box, index * PAN_DEV, PAN_DEV, 0)
        weights = lax.dynamic_slice_in_dim(radiation, index * PAN_DEV, PAN_DEV, 0)
        return aggregate_block(signal, owner, weights)

    outgoing = lax.map(outgoing_block, jnp.arange(N_DOM, dtype=jnp.int32))
    outgoing = jnp.transpose(outgoing, (1, 0, 2, 3)).reshape(TS, B, K)
    used = (jnp.arange(J, dtype=jnp.int32)[None, :] < list_count[:, None])

    def direction_block(index):
        first = index * 32
        rays = lax.dynamic_slice_in_dim(outgoing, first, 32, 2)
        kernel = lax.dynamic_slice_in_dim(translation, first, 32, 2)
        lag_kernel = jnp.transpose(kernel, (1, 0, 2))[:, list_class, :] * used[None, :, :, None].astype(kernel.dtype)
        gathered = rays[:, list_source, :]
        result = []
        for step_out in range(TS):
            total = jnp.zeros((B, 32), jnp.float32)
            for step_in in range(step_out + 1):
                total = total + jnp.sum(lag_kernel[step_out - step_in].astype(jnp.float32) * gathered[step_in].astype(jnp.float32), axis=1)
            result.append(total.astype(jnp.bfloat16))
        return jnp.stack(result)

    incoming = lax.map(direction_block, jnp.arange(K // 32, dtype=jnp.int32))
    incoming = jnp.transpose(incoming, (1, 2, 0, 3)).reshape(TS, B, K)

    def field_block(index):
        rays = lax.dynamic_slice_in_dim(incoming, index * BOX_DEV, BOX_DEV, 1)
        owner = lax.dynamic_slice_in_dim(panel_box, index * PAN_DEV, PAN_DEV, 0)
        weights = lax.dynamic_slice_in_dim(reception, index * PAN_DEV, PAN_DEV, 0)
        partial_value = lax.dot_general(rays.reshape(TS * BOX_DEV, K), weights, (((1,), (1,)), ((), ())), preferred_element_type=jnp.float32)
        partial_value = partial_value.reshape(TS, BOX_DEV, PAN_DEV)
        box_onehot = (owner[None, :] == jnp.arange(BOX_DEV, dtype=jnp.int32)[:, None]).astype(jnp.float32)
        return jnp.sum(partial_value * box_onehot[None], axis=1).astype(jnp.bfloat16)

    field = lax.map(field_block, jnp.arange(N_DOM, dtype=jnp.int32))
    return jnp.transpose(field, (1, 0, 2)).reshape(TS, PAN)
```

```python
import functools
import math

import jax
import jax.numpy as jnp
from jax import lax
from jax.experimental import pallas as pl
from jax.experimental.pallas import tpu as pltpu
from jax.sharding import PartitionSpec as P

def lag_sum(kern_rows, gathered, out_steps, offset):
    entries = kern_rows.shape[0]
    lags_all = kern_rows.shape[1]
    width = kern_rows.shape[2]
    results = []
    for step_out in range(out_steps):
        total = jnp.zeros((entries, width), jnp.float32)
        for step_in in range(gathered.shape[1]):
            delay = offset + step_out - step_in
            picked = lax.dynamic_index_in_dim(
                kern_rows, jnp.clip(delay, 0, lags_all - 1), 1, keepdims=False
            )
            weight = jnp.where(delay >= 0, picked.astype(jnp.float32), 0.0)
            total = total + weight * gathered[:, step_in].astype(jnp.float32)
        results.append(total)
    return jnp.stack(results, axis=1)


def body(
    panel_signal, panel_box, radiation, reception, translation, list_source, list_class, list_count
):
    rows_own = panel_signal.shape[0]
    dirs_own = translation.shape[2]
    boxes_all = list_source.shape[0]
    classes_all = translation.shape[0]
    lags_all = translation.shape[1]
    BOX_DEV = boxes_all // lax.axis_size("dom")
    J = list_source.shape[1]
    box_onehot = (panel_box[None, :] == jnp.arange(BOX_DEV, dtype=jnp.int32)[:, None]).astype(
        jnp.bfloat16
    )
    used_rows = (jnp.arange(J, dtype=jnp.int32)[None, :] < list_count[:, None]).astype(jnp.bfloat16)
    block_size = math.gcd(boxes_all, 256)

    def translate_all(table, rays, out_steps, offset):
        width = table.shape[2]
        count_in = rays.shape[1]
        flat_table = table.reshape(classes_all, lags_all * width)
        flat_rays = rays.reshape(boxes_all, count_in * width)

        def one_block(index):
            sources = lax.dynamic_slice_in_dim(
                list_source, index * block_size, block_size, 0
            ).reshape(block_size * J)
            classes = lax.dynamic_slice_in_dim(
                list_class, index * block_size, block_size, 0
            ).reshape(block_size * J)
            keep_rows = lax.dynamic_slice_in_dim(
                used_rows, index * block_size, block_size, 0
            ).reshape(block_size * J, 1)
            kern_rows = (jnp.take(flat_table, classes, axis=0) * keep_rows).reshape(
                block_size * J, lags_all, width
            )
            gathered = jnp.take(flat_rays, sources, axis=0).reshape(block_size * J, count_in, width)
            summed = lag_sum(kern_rows, gathered, out_steps, offset)
            return jnp.sum(summed.reshape(block_size, J, out_steps, width), axis=1)

        blocks = lax.map(one_block, jnp.arange(boxes_all // block_size, dtype=jnp.int32))
        return blocks.reshape(boxes_all, out_steps, width)

    masked = panel_signal[:, None, :] * box_onehot[None]
    outgoing = jnp.einsum(
        "rbp,pk->brk", masked, radiation, preferred_element_type=jnp.float32
    ).astype(jnp.bfloat16)
    spread = lax.all_to_all(outgoing, "dom", split_axis=2, concat_axis=0, tiled=True)
    first = lax.axis_index("tm") * rows_own
    empty = jnp.zeros((boxes_all, rows_own, dirs_own), jnp.float32)
    piece = lax.all_gather(spread, "tm", axis=1, tiled=True)

    def active():
        return empty + translate_all(translation, piece, rows_own, first)

    def passive():
        return empty

    incoming = lax.cond(jnp.int32(0) <= first + rows_own - 1, active, passive)
    rays = lax.all_to_all(
        incoming.astype(jnp.bfloat16), "dom", split_axis=0, concat_axis=2, tiled=True
    )
    partial_value = jnp.einsum("brk,pk->brp", rays, reception, preferred_element_type=jnp.float32)
    field = jnp.sum(partial_value * box_onehot.astype(jnp.float32)[:, None, :], axis=0)
    return field.astype(jnp.bfloat16)


LANES = 128
SUBLANES = 8
MESH = pl.DeviceIdType.MESH


def flips(mine, count):
    bits, bit = [], 1
    while bit < count:
        bits.append((bit, lax.rem(lax.div(mine, bit), 2)))
        bit *= 2
    found = []
    for mask in range(count):
        total = jnp.int32(0)
        for bit, value in bits:
            total = total + bit * ((1 - value) if mask & bit else value)
        found.append(total)
    return found


def spin(values, shift):
    shift = shift % LANES
    return values if shift == 0 else pltpu.roll(values, shift, 1)


def swap_groups(tiles, lane_group):
    count = len(tiles)
    span = LANES // count
    tiles = list(tiles)
    width = count // 2
    while width:
        low = (lane_group // width) % 2 == 0
        swapped = list(tiles)
        for index in range(count):
            if (index // width) % 2:
                continue
            first, second = tiles[index], tiles[index + width]
            if width * 2 == count:
                moved = spin(jnp.where(low, second, first), width * span)
                swapped[index] = jnp.where(low, first, moved)
                swapped[index + width] = jnp.where(low, moved, second)
            else:
                swapped[index] = jnp.where(low, first, spin(second, width * span))
                swapped[index + width] = jnp.where(low, spin(first, -width * span), second)
        tiles = swapped
        width //= 2
    return tiles


def sum_groups(sums, lane_group):
    count = len(sums)
    span = LANES // count
    width = count
    while width > 1:
        width //= 2
        low = (lane_group // width) % 2 == 0
        merged = []
        for part in range(width):
            first, second = sums[part], sums[part + width]
            if width * 2 == count:
                moved = spin(jnp.where(low, second, first), width * span)
            else:
                moved = jnp.where(low, spin(first, -width * span), spin(second, width * span))
            merged.append(jnp.where(low, first, second) + moved)
        sums = merged
    return sums[0]


def kernel(
    n_dom,
    n_tm,
    signal_hbm,
    box_hbm,
    rad_hbm,
    rec_hbm,
    trans_hbm,
    source_hbm,
    class_hbm,
    count_hbm,
    out_ref,
    signal_ref,
    box_ref,
    source_ref,
    class_ref,
    count_ref,
    rad,
    rec,
    trans,
    trans_wide,
    table,
    pick_source,
    pick_class,
    kern,
    rays,
    send_out,
    recv_out,
    send_in,
    recv_in,
    small_sem,
    load_sem,
    out_send_sem,
    out_recv_sem,
    in_send_sem,
    in_recv_sem,
):
    n_dev = n_dom * n_tm
    dom, tm = lax.axis_index("dom"), lax.axis_index("tm")
    steps_own, panels = signal_ref.shape
    dirs_all = rad.shape[1]
    classes, lags, _ = trans.shape
    entries, boxes_all = source_ref.shape
    boxes_own = boxes_all // n_dom
    span = LANES // n_tm
    rows_all = n_tm * SUBLANES
    chunks = load_sem.shape[0] - 2
    depth = panels // chunks
    dom_of = flips(dom, n_dom)
    tm_of = flips(tm, n_tm)
    peers = range(n_dev - 1, 0, -1)

    def place(mask):
        return {"dom": dom_of[mask // n_tm], "tm": tm_of[mask % n_tm]}

    def rad_copy(index):
        at = pl.ds(index * depth, depth)
        return pltpu.make_async_copy(rad_hbm.at[at, :], rad.at[at, :], load_sem.at[index])

    rec_copy = pltpu.make_async_copy(rec_hbm, rec, load_sem.at[chunks])
    trans_copy = pltpu.make_async_copy(trans_hbm, trans, load_sem.at[chunks + 1])
    small = [
        pltpu.make_async_copy(source, target, small_sem.at[index])
        for index, (source, target) in enumerate(
            [
                (signal_hbm, signal_ref),
                (box_hbm, box_ref),
                (source_hbm, source_ref),
                (class_hbm, class_ref),
                (count_hbm, count_ref),
            ]
        )
    ]

    barrier = pltpu.get_barrier_semaphore()
    small[0].start()
    small[1].start()
    for index in range(chunks):
        rad_copy(index).start()
    for mask in peers:
        pl.semaphore_signal(barrier, inc=1, device_id=place(mask), device_id_type=MESH)
    trans_copy.start()
    for copy in small[2:]:
        copy.start()
    rec_copy.start()
    small[0].wait()
    small[1].wait()

    lane_group = lax.broadcasted_iota(jnp.int32, (SUBLANES, LANES), 1) // span

    row = lax.broadcasted_iota(jnp.int32, (rows_all, panels), 0)
    row_box = row // (steps_own * SUBLANES) * SUBLANES + row % SUBLANES
    row_step = (row // SUBLANES) % steps_own
    owned = box_ref[...] == row_box
    signal = signal_ref[...].astype(jnp.float32)
    spread = signal[0:1]
    for step in range(1, steps_own):
        spread = jnp.where(row_step == step, signal[step : step + 1], spread)
    masked = jnp.where(owned, spread, 0.0).astype(jnp.bfloat16)

    outgoing = jnp.zeros((rows_all, dirs_all), jnp.float32)
    for index in range(chunks):
        rad_copy(index).wait()
        outgoing = outgoing + jnp.dot(
            masked[:, index * depth : (index + 1) * depth],
            rad[index * depth : (index + 1) * depth, :],
            preferred_element_type=jnp.float32,
        )
    for owner in range(n_dom):
        tiles = [
            outgoing[part * SUBLANES : (part + 1) * SUBLANES, owner * LANES : (owner + 1) * LANES]
            for part in range(n_tm)
        ]
        tiles = swap_groups(tiles, lane_group)
        for time in range(n_tm):
            send_out[dom_of[owner] * n_tm + tm_of[time]] = tiles[time].astype(jnp.bfloat16)

    pl.semaphore_wait(barrier, n_dev - 1)

    def out_copy(mask):
        return pltpu.make_async_remote_copy(
            src_ref=send_out.at[mask],
            dst_ref=recv_out.at[mask],
            send_sem=out_send_sem.at[mask],
            recv_sem=out_recv_sem.at[mask],
            device_id=place(mask),
            device_id_type=MESH,
        )

    def in_copy(mask):
        return pltpu.make_async_remote_copy(
            src_ref=send_in.at[mask],
            dst_ref=recv_in.at[mask],
            send_sem=in_send_sem.at[mask],
            recv_sem=in_recv_sem.at[mask],
            device_id=place(mask),
            device_id_type=MESH,
        )

    for mask in peers:
        out_copy(mask).start()
    recv_out[0] = send_out[0]

    trans_copy.wait()
    trans_wide[...] = trans[...].astype(jnp.float32).reshape(classes * lags, LANES)
    for index in range(classes // (2 * SUBLANES)):
        columns = [[] for _ in range(2 * n_tm)]
        for part in range(2):
            base = (2 * index + part) * SUBLANES * lags
            wide = []
            for lag in range(lags):
                tile = trans_wide[pl.ds(base + lag, SUBLANES, stride=lags), :]
                tile = jnp.where(lane_group == tm, tile, 0.0)
                shift = span
                while shift < LANES:
                    tile = tile + spin(tile, shift)
                    shift *= 2
                wide.append(tile)
            for turn in range(n_tm):
                for half in range(2):
                    tile = jnp.zeros_like(wide[0])
                    for group in range(n_tm):
                        if half == 0 or group <= turn:
                            lag = half * n_tm + (turn - group) % n_tm
                            tile = jnp.where(lane_group == group, wide[lag], tile)
                    columns[2 * turn + half].append(tile)
        at = pl.ds(index * 2 * SUBLANES, 2 * SUBLANES)
        for column, parts in enumerate(columns):
            table[at, column * LANES : (column + 1) * LANES] = jnp.concatenate(
                parts, axis=0
            ).astype(jnp.bfloat16)

    for copy in small[2:]:
        copy.wait()
    used = lax.broadcasted_iota(jnp.int32, class_ref.shape, 0) < count_ref[...]
    kinds = jnp.where(used, class_ref[...], classes).astype(jnp.float32).T
    sources = source_ref[...].astype(jnp.float32).T
    lane = lax.broadcasted_iota(jnp.int32, (boxes_all, LANES), 1).astype(jnp.float32)
    for entry in range(entries):
        pick_class[entry] = jnp.where(
            kinds[:, entry : entry + 1] == lane[:, :classes], 1.0, 0.0
        ).astype(jnp.bfloat16)
        pick_source[entry] = jnp.where(sources[:, entry : entry + 1] == lane, 1.0, 0.0).astype(
            jnp.bfloat16
        )
    for entry in range(entries):
        rows = jnp.dot(pick_class[entry], table[...], preferred_element_type=jnp.float32)
        for column in range(2 * n_tm):
            kern[column, entry * boxes_all : (entry + 1) * boxes_all, :] = rows[
                :, column * LANES : (column + 1) * LANES
            ]

    for mask in range(n_dom):
        tiles = []
        for part in range(n_tm):
            if mask or part:
                out_copy(mask * n_tm + part).wait_recv()
        for time in range(n_tm):
            tiles.append(recv_out[mask * n_tm + tm_of[time]].astype(jnp.float32))
        at = pl.ds(pl.multiple_of(dom_of[mask] * boxes_own, boxes_own), boxes_own)
        low = lane_group < n_tm // 2
        for half in range(2):
            first, second = tiles[2 * half], tiles[2 * half + 1]
            upper = jnp.where(low, first, spin(second, LANES // 2))
            lower = jnp.where(low, spin(first, LANES // 2), second)
            rays[at, half * LANES : (half + 1) * LANES] = jnp.concatenate(
                [upper, lower], axis=0
            ).astype(jnp.bfloat16)

    for mask in range(n_dom - 1, -1, -1):
        first_box = pl.multiple_of(dom_of[mask] * boxes_own, boxes_own)
        picked = jnp.concatenate(
            [pick_source[entry, pl.ds(first_box, boxes_own), :] for entry in range(entries)], axis=0
        )
        found = jnp.dot(picked, rays[...], preferred_element_type=jnp.float32)
        totals = []
        for part in range(2):
            total = [None] * (2 * n_tm)
            for entry in range(entries):
                at = entry * boxes_own + part * SUBLANES
                early = found[at : at + SUBLANES, :LANES]
                late = found[at : at + SUBLANES, LANES:]
                rows = pl.ds(entry * boxes_all + first_box + part * SUBLANES, SUBLANES)
                for turn in range(n_tm):
                    near = kern[2 * turn, rows, :]
                    far = kern[2 * turn + 1, rows, :]
                    if turn == n_tm - 1:
                        young, old = early, late
                    else:
                        young = jnp.where(lane_group <= turn, early, 0.0)
                        old = jnp.where(lane_group <= turn, late, early)
                    adds = [near * young, near * old + far * early]
                    for half in range(2):
                        at_step = half * n_tm + turn
                        total[at_step] = (
                            adds[half] if entry == 0 else total[at_step] + adds[half]
                        )
            totals.append(total)
        for time in range(n_tm):
            sums = [
                totals[part][time * steps_own + step]
                for part in range(2)
                for step in range(steps_own)
            ]
            send_in[mask * n_tm + tm_of[time]] = sum_groups(sums, lane_group).astype(jnp.bfloat16)
        for part in range(n_tm - 1, -1, -1):
            if mask or part:
                in_copy(mask * n_tm + part).start()
    recv_in[0] = send_in[0]

    rec_copy.wait()
    field = jnp.zeros((rows_all, panels), jnp.float32)
    for mask in range(n_dom):
        for part in range(n_tm):
            if mask or part:
                in_copy(mask * n_tm + part).wait_recv()
        tiles = [recv_in[mask * n_tm + tm_of[time]].astype(jnp.float32) for time in range(n_tm)]
        incoming = jnp.concatenate(swap_groups(tiles, lane_group), axis=0).astype(jnp.bfloat16)
        field = field + lax.dot_general(
            incoming,
            rec[:, pl.ds(pl.multiple_of(dom_of[mask] * LANES, LANES), LANES)],
            (((1,), (1,)), ((), ())),
            preferred_element_type=jnp.float32,
        )
    chosen = jnp.where(owned, field, 0.0)
    for step in range(steps_own):
        mine = jnp.where(row_step == step, chosen, 0.0)
        out_ref[step : step + 1, :] = jnp.sum(mine, axis=0, keepdims=True).astype(out_ref.dtype)

    for mask in peers:
        out_copy(mask).wait_send()
        in_copy(mask).wait_send()


def fused_body(
    n_dom,
    n_tm,
    panel_signal,
    panel_box,
    radiation,
    reception,
    translation,
    list_source,
    list_class,
    list_count,
):
    steps_own, panels = panel_signal.shape
    dirs_all = radiation.shape[1]
    classes, lags, _ = translation.shape
    boxes_all, entries = list_source.shape
    n_dev = n_dom * n_tm
    chunks = 4
    vmem = pl.BlockSpec(memory_space=pltpu.VMEM)
    hbm = pl.BlockSpec(memory_space=pl.ANY)
    message = pltpu.VMEM((n_dev, SUBLANES, LANES), jnp.bfloat16)
    lists = pltpu.VMEM((entries, boxes_all), jnp.int32)
    return pl.pallas_call(
        functools.partial(kernel, n_dom, n_tm),
        out_shape=jax.ShapeDtypeStruct((steps_own, panels), jnp.bfloat16),
        in_specs=[hbm] * 8,
        out_specs=vmem,
        scratch_shapes=[
            pltpu.VMEM((steps_own, panels), jnp.bfloat16),
            pltpu.VMEM((1, panels), jnp.int32),
            lists,
            lists,
            pltpu.VMEM((1, boxes_all), jnp.int32),
            pltpu.VMEM((panels, dirs_all), jnp.bfloat16),
            pltpu.VMEM((panels, dirs_all), jnp.bfloat16),
            pltpu.VMEM(translation.shape, jnp.bfloat16),
            pltpu.VMEM((classes * lags, LANES), jnp.float32),
            pltpu.VMEM((classes, lags * LANES), jnp.bfloat16),
            pltpu.VMEM((entries, boxes_all, boxes_all), jnp.bfloat16),
            pltpu.VMEM((entries, boxes_all, classes), jnp.bfloat16),
            pltpu.VMEM((lags, entries * boxes_all, LANES), jnp.float32),
            pltpu.VMEM((boxes_all, 2 * LANES), jnp.bfloat16),
            message,
            message,
            message,
            message,
            pltpu.SemaphoreType.DMA((5,)),
            pltpu.SemaphoreType.DMA((chunks + 2,)),
            pltpu.SemaphoreType.DMA((n_dev,)),
            pltpu.SemaphoreType.DMA((n_dev,)),
            pltpu.SemaphoreType.DMA((n_dev,)),
            pltpu.SemaphoreType.DMA((n_dev,)),
        ],
        compiler_params=pltpu.CompilerParams(
            collective_id=0, has_side_effects=True, vmem_limit_bytes=48 * 1024 * 1024
        ),
    )(
        panel_signal,
        panel_box.reshape(1, panels),
        radiation,
        reception,
        translation,
        list_source.T,
        list_class.T,
        list_count.reshape(1, boxes_all),
    )


def whole_body(n_dom, n_tm, *args):
    panel_signal, translation, boxes_all = args[0], args[4], args[5].shape[0]
    steps_own = panel_signal.shape[0]
    classes, lags, dirs_own = translation.shape
    boxes_own = boxes_all // n_dom
    fits = (
        dirs_own == LANES
        and boxes_all == LANES
        and n_dom & (n_dom - 1) == 0
        and n_tm & (n_tm - 1) == 0
        and lags == 2 * n_tm
        and steps_own * n_tm == lags
        and boxes_own == 2 * SUBLANES
        and steps_own * boxes_own == n_tm * SUBLANES
        and classes % (2 * SUBLANES) == 0
        and classes <= LANES
    )
    if fits:
        return fused_body(n_dom, n_tm, *args)
    return body(*args)


def solution(mesh):
    placed = (
        P("tm", "dom"),
        P("dom"),
        P("dom", None),
        P("dom", None),
        P(None, None, "dom"),
        P(),
        P(),
        P(),
    )
    return jax.shard_map(
        functools.partial(whole_body, mesh.shape["dom"], mesh.shape["tm"]),
        mesh=mesh, in_specs=placed, out_specs=P("tm", "dom"), check_vma=False
    )
```

```python
import functools
import math

import jax
import jax.numpy as jnp
from jax import lax
from jax.experimental import pallas as pl
from jax.experimental.pallas import tpu as pltpu
from jax.sharding import PartitionSpec as P

def lag_sum(kern_rows, gathered, out_steps, offset):
    entries = kern_rows.shape[0]
    lags_all = kern_rows.shape[1]
    width = kern_rows.shape[2]
    results = []
    for step_out in range(out_steps):
        total = jnp.zeros((entries, width), jnp.float32)
        for step_in in range(gathered.shape[1]):
            delay = offset + step_out - step_in
            picked = lax.dynamic_index_in_dim(
                kern_rows, jnp.clip(delay, 0, lags_all - 1), 1, keepdims=False
            )
            weight = jnp.where(delay >= 0, picked.astype(jnp.float32), 0.0)
            total = total + weight * gathered[:, step_in].astype(jnp.float32)
        results.append(total)
    return jnp.stack(results, axis=1)


def body(
    panel_signal, panel_box, radiation, reception, translation, list_source, list_class, list_count
):
    rows_own = panel_signal.shape[0]
    dirs_own = translation.shape[2]
    boxes_all = list_source.shape[0]
    classes_all = translation.shape[0]
    lags_all = translation.shape[1]
    BOX_DEV = boxes_all // lax.axis_size("dom")
    J = list_source.shape[1]
    box_onehot = (panel_box[None, :] == jnp.arange(BOX_DEV, dtype=jnp.int32)[:, None]).astype(
        jnp.bfloat16
    )
    used_rows = (jnp.arange(J, dtype=jnp.int32)[None, :] < list_count[:, None]).astype(jnp.bfloat16)
    block_size = math.gcd(boxes_all, 256)

    def translate_all(table, rays, out_steps, offset):
        width = table.shape[2]
        count_in = rays.shape[1]
        flat_table = table.reshape(classes_all, lags_all * width)
        flat_rays = rays.reshape(boxes_all, count_in * width)

        def one_block(index):
            sources = lax.dynamic_slice_in_dim(
                list_source, index * block_size, block_size, 0
            ).reshape(block_size * J)
            classes = lax.dynamic_slice_in_dim(
                list_class, index * block_size, block_size, 0
            ).reshape(block_size * J)
            keep_rows = lax.dynamic_slice_in_dim(
                used_rows, index * block_size, block_size, 0
            ).reshape(block_size * J, 1)
            kern_rows = (jnp.take(flat_table, classes, axis=0) * keep_rows).reshape(
                block_size * J, lags_all, width
            )
            gathered = jnp.take(flat_rays, sources, axis=0).reshape(block_size * J, count_in, width)
            summed = lag_sum(kern_rows, gathered, out_steps, offset)
            return jnp.sum(summed.reshape(block_size, J, out_steps, width), axis=1)

        blocks = lax.map(one_block, jnp.arange(boxes_all // block_size, dtype=jnp.int32))
        return blocks.reshape(boxes_all, out_steps, width)

    masked = panel_signal[:, None, :] * box_onehot[None]
    outgoing = jnp.einsum(
        "rbp,pk->brk", masked, radiation, preferred_element_type=jnp.float32
    ).astype(jnp.bfloat16)
    spread = lax.all_to_all(outgoing, "dom", split_axis=2, concat_axis=0, tiled=True)
    first = lax.axis_index("tm") * rows_own
    empty = jnp.zeros((boxes_all, rows_own, dirs_own), jnp.float32)
    piece = lax.all_gather(spread, "tm", axis=1, tiled=True)

    def active():
        return empty + translate_all(translation, piece, rows_own, first)

    def passive():
        return empty

    incoming = lax.cond(jnp.int32(0) <= first + rows_own - 1, active, passive)
    rays = lax.all_to_all(
        incoming.astype(jnp.bfloat16), "dom", split_axis=0, concat_axis=2, tiled=True
    )
    partial_value = jnp.einsum("brk,pk->brp", rays, reception, preferred_element_type=jnp.float32)
    field = jnp.sum(partial_value * box_onehot.astype(jnp.float32)[:, None, :], axis=0)
    return field.astype(jnp.bfloat16)


LANES = 128
SUBLANES = 8
MESH = pl.DeviceIdType.MESH


def flips(mine, count):
    bits, bit = [], 1
    while bit < count:
        bits.append((bit, lax.rem(lax.div(mine, bit), 2)))
        bit *= 2
    found = []
    for mask in range(count):
        total = jnp.int32(0)
        for bit, value in bits:
            total = total + bit * ((1 - value) if mask & bit else value)
        found.append(total)
    return found


def spin(values, shift):
    shift = shift % LANES
    return values if shift == 0 else pltpu.roll(values, shift, 1)


def swap_groups(tiles, lane_group):
    count = len(tiles)
    span = LANES // count
    tiles = list(tiles)
    width = count // 2
    while width:
        low = (lane_group // width) % 2 == 0
        swapped = list(tiles)
        for index in range(count):
            if (index // width) % 2:
                continue
            first, second = tiles[index], tiles[index + width]
            if width * 2 == count:
                moved = spin(jnp.where(low, second, first), width * span)
                swapped[index] = jnp.where(low, first, moved)
                swapped[index + width] = jnp.where(low, moved, second)
            else:
                swapped[index] = jnp.where(low, first, spin(second, width * span))
                swapped[index + width] = jnp.where(low, spin(first, -width * span), second)
        tiles = swapped
        width //= 2
    return tiles


def sum_groups(sums, lane_group):
    count = len(sums)
    span = LANES // count
    width = count
    while width > 1:
        width //= 2
        low = (lane_group // width) % 2 == 0
        merged = []
        for part in range(width):
            first, second = sums[part], sums[part + width]
            if width * 2 == count:
                moved = spin(jnp.where(low, second, first), width * span)
            else:
                moved = jnp.where(low, spin(first, -width * span), spin(second, width * span))
            merged.append(jnp.where(low, first, second) + moved)
        sums = merged
    return sums[0]


def kernel(
    n_dom,
    n_tm,
    signal_hbm,
    box_hbm,
    rad_hbm,
    rec_hbm,
    trans_hbm,
    source_hbm,
    class_hbm,
    count_hbm,
    out_ref,
    signal_ref,
    box_ref,
    source_ref,
    class_ref,
    count_ref,
    rad,
    rec,
    trans,
    trans_wide,
    table,
    pick_source,
    pick_class,
    kern,
    rays,
    send_out,
    recv_out,
    send_in,
    recv_in,
    small_sem,
    load_sem,
    out_send_sem,
    out_recv_sem,
    in_send_sem,
    in_recv_sem,
):
    n_dev = n_dom * n_tm
    dom, tm = lax.axis_index("dom"), lax.axis_index("tm")
    steps_own, panels = signal_ref.shape
    dirs_all = rad.shape[1]
    classes, lags, _ = trans.shape
    entries, boxes_all = source_ref.shape
    boxes_own = boxes_all // n_dom
    span = LANES // n_tm
    rows_all = n_tm * SUBLANES
    chunks = load_sem.shape[0] - 2
    depth = panels // chunks
    dom_of = flips(dom, n_dom)
    tm_of = flips(tm, n_tm)
    peers = range(n_dev - 1, 0, -1)

    def place(mask):
        return {"dom": dom_of[mask // n_tm], "tm": tm_of[mask % n_tm]}

    def rad_copy(index):
        at = pl.ds(index * depth, depth)
        return pltpu.make_async_copy(rad_hbm.at[at, :], rad.at[at, :], load_sem.at[index])

    rec_copy = pltpu.make_async_copy(rec_hbm, rec, load_sem.at[chunks])
    trans_copy = pltpu.make_async_copy(trans_hbm, trans, load_sem.at[chunks + 1])
    small = [
        pltpu.make_async_copy(source, target, small_sem.at[index])
        for index, (source, target) in enumerate(
            [
                (signal_hbm, signal_ref),
                (box_hbm, box_ref),
                (source_hbm, source_ref),
                (class_hbm, class_ref),
                (count_hbm, count_ref),
            ]
        )
    ]

    barrier = pltpu.get_barrier_semaphore()
    small[0].start()
    small[1].start()
    for index in range(chunks):
        rad_copy(index).start()
    for mask in peers:
        pl.semaphore_signal(barrier, inc=1, device_id=place(mask), device_id_type=MESH)
    trans_copy.start()
    for copy in small[2:]:
        copy.start()
    rec_copy.start()
    small[0].wait()
    small[1].wait()

    lane_group = lax.broadcasted_iota(jnp.int32, (SUBLANES, LANES), 1) // span

    row = lax.broadcasted_iota(jnp.int32, (rows_all, panels), 0)
    row_box = row // (steps_own * SUBLANES) * SUBLANES + row % SUBLANES
    row_step = (row // SUBLANES) % steps_own
    owned = box_ref[...] == row_box
    signal = signal_ref[...].astype(jnp.float32)
    spread = signal[0:1]
    for step in range(1, steps_own):
        spread = jnp.where(row_step == step, signal[step : step + 1], spread)
    masked = jnp.where(owned, spread, 0.0).astype(jnp.bfloat16)

    outgoing = jnp.zeros((rows_all, dirs_all), jnp.float32)
    for index in range(chunks):
        rad_copy(index).wait()
        outgoing = outgoing + jnp.dot(
            masked[:, index * depth : (index + 1) * depth],
            rad[index * depth : (index + 1) * depth, :],
            preferred_element_type=jnp.float32,
        )
    for owner in range(n_dom):
        tiles = [
            outgoing[part * SUBLANES : (part + 1) * SUBLANES, owner * LANES : (owner + 1) * LANES]
            for part in range(n_tm)
        ]
        tiles = swap_groups(tiles, lane_group)
        for time in range(n_tm):
            send_out[dom_of[owner] * n_tm + tm_of[time]] = tiles[time].astype(jnp.bfloat16)

    pl.semaphore_wait(barrier, n_dev - 1)

    def out_copy(mask):
        return pltpu.make_async_remote_copy(
            src_ref=send_out.at[mask],
            dst_ref=recv_out.at[mask],
            send_sem=out_send_sem.at[mask],
            recv_sem=out_recv_sem.at[mask],
            device_id=place(mask),
            device_id_type=MESH,
        )

    def in_copy(mask):
        return pltpu.make_async_remote_copy(
            src_ref=send_in.at[mask],
            dst_ref=recv_in.at[mask],
            send_sem=in_send_sem.at[mask],
            recv_sem=in_recv_sem.at[mask],
            device_id=place(mask),
            device_id_type=MESH,
        )

    for mask in peers:
        out_copy(mask).start()
    recv_out[0] = send_out[0]

    trans_copy.wait()
    trans_wide[...] = trans[...].astype(jnp.float32).reshape(classes * lags, LANES)
    for index in range(classes // (2 * SUBLANES)):
        columns = [[] for _ in range(2 * n_tm)]
        for part in range(2):
            base = (2 * index + part) * SUBLANES * lags
            wide = []
            for lag in range(lags):
                tile = trans_wide[pl.ds(base + lag, SUBLANES, stride=lags), :]
                tile = jnp.where(lane_group == tm, tile, 0.0)
                shift = span
                while shift < LANES:
                    tile = tile + spin(tile, shift)
                    shift *= 2
                wide.append(tile)
            for turn in range(n_tm):
                for half in range(2):
                    tile = jnp.zeros_like(wide[0])
                    for group in range(n_tm):
                        if half == 0 or group <= turn:
                            lag = half * n_tm + (turn - group) % n_tm
                            tile = jnp.where(lane_group == group, wide[lag], tile)
                    columns[2 * turn + half].append(tile)
        at = pl.ds(index * 2 * SUBLANES, 2 * SUBLANES)
        for column, parts in enumerate(columns):
            table[at, column * LANES : (column + 1) * LANES] = jnp.concatenate(
                parts, axis=0
            ).astype(jnp.bfloat16)

    for copy in small[2:]:
        copy.wait()
    used = lax.broadcasted_iota(jnp.int32, class_ref.shape, 0) < count_ref[...]
    kinds = jnp.where(used, class_ref[...], classes).astype(jnp.float32).T
    sources = source_ref[...].astype(jnp.float32).T
    lane = lax.broadcasted_iota(jnp.int32, (boxes_all, LANES), 1).astype(jnp.float32)
    for entry in range(entries):
        pick_class[entry] = jnp.where(
            kinds[:, entry : entry + 1] == lane[:, :classes], 1.0, 0.0
        ).astype(jnp.bfloat16)
        pick_source[entry] = jnp.where(sources[:, entry : entry + 1] == lane, 1.0, 0.0).astype(
            jnp.bfloat16
        )
    for entry in range(entries):
        rows = jnp.dot(pick_class[entry], table[...], preferred_element_type=jnp.float32)
        for column in range(2 * n_tm):
            kern[column, entry * boxes_all : (entry + 1) * boxes_all, :] = rows[
                :, column * LANES : (column + 1) * LANES
            ]

    for mask in range(n_dom):
        tiles = []
        for part in range(n_tm):
            if mask or part:
                out_copy(mask * n_tm + part).wait_recv()
        for time in range(n_tm):
            tiles.append(recv_out[mask * n_tm + tm_of[time]].astype(jnp.float32))
        at = pl.ds(pl.multiple_of(dom_of[mask] * boxes_own, boxes_own), boxes_own)
        low = lane_group < n_tm // 2
        for half in range(2):
            first, second = tiles[2 * half], tiles[2 * half + 1]
            upper = jnp.where(low, first, spin(second, LANES // 2))
            lower = jnp.where(low, spin(first, LANES // 2), second)
            rays[at, half * LANES : (half + 1) * LANES] = jnp.concatenate(
                [upper, lower], axis=0
            ).astype(jnp.bfloat16)

    for mask in range(n_dom - 1, -1, -1):
        first_box = pl.multiple_of(dom_of[mask] * boxes_own, boxes_own)
        picked = jnp.concatenate(
            [pick_source[entry, pl.ds(first_box, boxes_own), :] for entry in range(entries)], axis=0
        )
        found = jnp.dot(picked, rays[...], preferred_element_type=jnp.float32)
        totals = []
        for part in range(2):
            total = [None] * (2 * n_tm)
            for entry in range(entries):
                at = entry * boxes_own + part * SUBLANES
                early = found[at : at + SUBLANES, :LANES]
                late = found[at : at + SUBLANES, LANES:]
                rows = pl.ds(entry * boxes_all + first_box + part * SUBLANES, SUBLANES)
                for turn in range(n_tm):
                    near = kern[2 * turn, rows, :]
                    far = kern[2 * turn + 1, rows, :]
                    if turn == n_tm - 1:
                        young, old = early, late
                    else:
                        young = jnp.where(lane_group <= turn, early, 0.0)
                        old = jnp.where(lane_group <= turn, late, early)
                    adds = [near * young, near * old + far * early]
                    for half in range(2):
                        at_step = half * n_tm + turn
                        total[at_step] = (
                            adds[half] if entry == 0 else total[at_step] + adds[half]
                        )
            totals.append(total)
        for time in range(n_tm):
            sums = [
                totals[part][time * steps_own + step]
                for part in range(2)
                for step in range(steps_own)
            ]
            send_in[mask * n_tm + tm_of[time]] = sum_groups(sums, lane_group).astype(jnp.bfloat16)
        for part in range(n_tm - 1, -1, -1):
            if mask or part:
                in_copy(mask * n_tm + part).start()
    recv_in[0] = send_in[0]

    rec_copy.wait()
    field = jnp.zeros((rows_all, panels), jnp.float32)
    for mask in range(n_dom):
        for part in range(n_tm):
            if mask or part:
                in_copy(mask * n_tm + part).wait_recv()
        tiles = [recv_in[mask * n_tm + tm_of[time]].astype(jnp.float32) for time in range(n_tm)]
        incoming = jnp.concatenate(swap_groups(tiles, lane_group), axis=0).astype(jnp.bfloat16)
        field = field + lax.dot_general(
            incoming,
            rec[:, pl.ds(pl.multiple_of(dom_of[mask] * LANES, LANES), LANES)],
            (((1,), (1,)), ((), ())),
            preferred_element_type=jnp.float32,
        )
    chosen = jnp.where(owned, field, 0.0)
    for step in range(steps_own):
        mine = jnp.where(row_step == step, chosen, 0.0)
        out_ref[step : step + 1, :] = jnp.sum(mine, axis=0, keepdims=True).astype(out_ref.dtype)

    for mask in peers:
        out_copy(mask).wait_send()
        in_copy(mask).wait_send()


def fused_body(
    n_dom,
    n_tm,
    panel_signal,
    panel_box,
    radiation,
    reception,
    translation,
    list_source,
    list_class,
    list_count,
):
    steps_own, panels = panel_signal.shape
    dirs_all = radiation.shape[1]
    classes, lags, _ = translation.shape
    boxes_all, entries = list_source.shape
    n_dev = n_dom * n_tm
    chunks = 4
    vmem = pl.BlockSpec(memory_space=pltpu.VMEM)
    hbm = pl.BlockSpec(memory_space=pl.ANY)
    message = pltpu.VMEM((n_dev, SUBLANES, LANES), jnp.bfloat16)
    lists = pltpu.VMEM((entries, boxes_all), jnp.int32)
    return pl.pallas_call(
        functools.partial(kernel, n_dom, n_tm),
        out_shape=jax.ShapeDtypeStruct((steps_own, panels), jnp.bfloat16),
        in_specs=[hbm] * 8,
        out_specs=vmem,
        scratch_shapes=[
            pltpu.VMEM((steps_own, panels), jnp.bfloat16),
            pltpu.VMEM((1, panels), jnp.int32),
            lists,
            lists,
            pltpu.VMEM((1, boxes_all), jnp.int32),
            pltpu.VMEM((panels, dirs_all), jnp.bfloat16),
            pltpu.VMEM((panels, dirs_all), jnp.bfloat16),
            pltpu.VMEM(translation.shape, jnp.bfloat16),
            pltpu.VMEM((classes * lags, LANES), jnp.float32),
            pltpu.VMEM((classes, lags * LANES), jnp.bfloat16),
            pltpu.VMEM((entries, boxes_all, boxes_all), jnp.bfloat16),
            pltpu.VMEM((entries, boxes_all, classes), jnp.bfloat16),
            pltpu.VMEM((lags, entries * boxes_all, LANES), jnp.float32),
            pltpu.VMEM((boxes_all, 2 * LANES), jnp.bfloat16),
            message,
            message,
            message,
            message,
            pltpu.SemaphoreType.DMA((5,)),
            pltpu.SemaphoreType.DMA((chunks + 2,)),
            pltpu.SemaphoreType.DMA((n_dev,)),
            pltpu.SemaphoreType.DMA((n_dev,)),
            pltpu.SemaphoreType.DMA((n_dev,)),
            pltpu.SemaphoreType.DMA((n_dev,)),
        ],
        compiler_params=pltpu.CompilerParams(
            collective_id=0, has_side_effects=True
        ),
    )(
        panel_signal,
        panel_box.reshape(1, panels),
        radiation,
        reception,
        translation,
        list_source.T,
        list_class.T,
        list_count.reshape(1, boxes_all),
    )


def whole_body(n_dom, n_tm, *args):
    panel_signal, translation, boxes_all = args[0], args[4], args[5].shape[0]
    steps_own = panel_signal.shape[0]
    classes, lags, dirs_own = translation.shape
    boxes_own = boxes_all // n_dom
    fits = (
        dirs_own == LANES
        and boxes_all == LANES
        and n_dom & (n_dom - 1) == 0
        and n_tm & (n_tm - 1) == 0
        and lags == 2 * n_tm
        and steps_own * n_tm == lags
        and boxes_own == 2 * SUBLANES
        and steps_own * boxes_own == n_tm * SUBLANES
        and classes % (2 * SUBLANES) == 0
        and classes <= LANES
    )
    if fits:
        return fused_body(n_dom, n_tm, *args)
    return body(*args)


def solution(mesh):
    placed = (
        P("tm", "dom"),
        P("dom"),
        P("dom", None),
        P("dom", None),
        P(None, None, "dom"),
        P(),
        P(),
        P(),
    )
    return jax.shard_map(
        functools.partial(whole_body, mesh.shape["dom"], mesh.shape["tm"]),
        mesh=mesh, in_specs=placed, out_specs=P("tm", "dom"), check_vma=False
    )
```

```python
import functools
import math

import jax
import jax.numpy as jnp
from jax import lax
from jax.experimental import pallas as pl
from jax.experimental.pallas import tpu as pltpu
from jax.sharding import PartitionSpec as P

def lag_sum(kern_rows, gathered, out_steps, offset):
    entries = kern_rows.shape[0]
    lags_all = kern_rows.shape[1]
    width = kern_rows.shape[2]
    results = []
    for step_out in range(out_steps):
        total = jnp.zeros((entries, width), jnp.float32)
        for step_in in range(gathered.shape[1]):
            delay = offset + step_out - step_in
            picked = lax.dynamic_index_in_dim(
                kern_rows, jnp.clip(delay, 0, lags_all - 1), 1, keepdims=False
            )
            weight = jnp.where(delay >= 0, picked.astype(jnp.float32), 0.0)
            total = total + weight * gathered[:, step_in].astype(jnp.float32)
        results.append(total)
    return jnp.stack(results, axis=1)


def body(
    panel_signal, panel_box, radiation, reception, translation, list_source, list_class, list_count
):
    rows_own = panel_signal.shape[0]
    dirs_own = translation.shape[2]
    boxes_all = list_source.shape[0]
    classes_all = translation.shape[0]
    lags_all = translation.shape[1]
    BOX_DEV = boxes_all // lax.axis_size("dom")
    J = list_source.shape[1]
    box_onehot = (panel_box[None, :] == jnp.arange(BOX_DEV, dtype=jnp.int32)[:, None]).astype(
        jnp.bfloat16
    )
    used_rows = (jnp.arange(J, dtype=jnp.int32)[None, :] < list_count[:, None]).astype(jnp.bfloat16)
    block_size = math.gcd(boxes_all, 256)

    def translate_all(table, rays, out_steps, offset):
        width = table.shape[2]
        count_in = rays.shape[1]
        flat_table = table.reshape(classes_all, lags_all * width)
        flat_rays = rays.reshape(boxes_all, count_in * width)

        def one_block(index):
            sources = lax.dynamic_slice_in_dim(
                list_source, index * block_size, block_size, 0
            ).reshape(block_size * J)
            classes = lax.dynamic_slice_in_dim(
                list_class, index * block_size, block_size, 0
            ).reshape(block_size * J)
            keep_rows = lax.dynamic_slice_in_dim(
                used_rows, index * block_size, block_size, 0
            ).reshape(block_size * J, 1)
            kern_rows = (jnp.take(flat_table, classes, axis=0) * keep_rows).reshape(
                block_size * J, lags_all, width
            )
            gathered = jnp.take(flat_rays, sources, axis=0).reshape(block_size * J, count_in, width)
            summed = lag_sum(kern_rows, gathered, out_steps, offset)
            return jnp.sum(summed.reshape(block_size, J, out_steps, width), axis=1)

        blocks = lax.map(one_block, jnp.arange(boxes_all // block_size, dtype=jnp.int32))
        return blocks.reshape(boxes_all, out_steps, width)

    masked = panel_signal[:, None, :] * box_onehot[None]
    outgoing = jnp.einsum(
        "rbp,pk->brk", masked, radiation, preferred_element_type=jnp.float32
    ).astype(jnp.bfloat16)
    spread = lax.all_to_all(outgoing, "dom", split_axis=2, concat_axis=0, tiled=True)
    first = lax.axis_index("tm") * rows_own
    empty = jnp.zeros((boxes_all, rows_own, dirs_own), jnp.float32)
    piece = lax.all_gather(spread, "tm", axis=1, tiled=True)

    def active():
        return empty + translate_all(translation, piece, rows_own, first)

    def passive():
        return empty

    incoming = lax.cond(jnp.int32(0) <= first + rows_own - 1, active, passive)
    rays = lax.all_to_all(
        incoming.astype(jnp.bfloat16), "dom", split_axis=0, concat_axis=2, tiled=True
    )
    partial_value = jnp.einsum("brk,pk->brp", rays, reception, preferred_element_type=jnp.float32)
    field = jnp.sum(partial_value * box_onehot.astype(jnp.float32)[:, None, :], axis=0)
    return field.astype(jnp.bfloat16)


LANES = 128
SUBLANES = 8
MESH = pl.DeviceIdType.MESH


def flips(mine, count):
    bits, bit = [], 1
    while bit < count:
        bits.append((bit, lax.rem(lax.div(mine, bit), 2)))
        bit *= 2
    found = []
    for mask in range(count):
        total = jnp.int32(0)
        for bit, value in bits:
            total = total + bit * ((1 - value) if mask & bit else value)
        found.append(total)
    return found


def spin(values, shift):
    shift = shift % LANES
    return values if shift == 0 else pltpu.roll(values, shift, 1)


def swap_groups(tiles, lane_group):
    count = len(tiles)
    span = LANES // count
    tiles = list(tiles)
    width = count // 2
    while width:
        low = (lane_group // width) % 2 == 0
        swapped = list(tiles)
        for index in range(count):
            if (index // width) % 2:
                continue
            first, second = tiles[index], tiles[index + width]
            if width * 2 == count:
                moved = spin(jnp.where(low, second, first), width * span)
                swapped[index] = jnp.where(low, first, moved)
                swapped[index + width] = jnp.where(low, moved, second)
            else:
                swapped[index] = jnp.where(low, first, spin(second, width * span))
                swapped[index + width] = jnp.where(low, spin(first, -width * span), second)
        tiles = swapped
        width //= 2
    return tiles


def sum_groups(sums, lane_group):
    count = len(sums)
    span = LANES // count
    width = count
    while width > 1:
        width //= 2
        low = (lane_group // width) % 2 == 0
        merged = []
        for part in range(width):
            first, second = sums[part], sums[part + width]
            if width * 2 == count:
                moved = spin(jnp.where(low, second, first), width * span)
            else:
                moved = jnp.where(low, spin(first, -width * span), spin(second, width * span))
            merged.append(jnp.where(low, first, second) + moved)
        sums = merged
    return sums[0]


def kernel(
    n_dom,
    n_tm,
    signal_hbm,
    box_hbm,
    rad_hbm,
    rec_hbm,
    trans_hbm,
    source_hbm,
    class_hbm,
    count_hbm,
    out_ref,
    signal_ref,
    box_ref,
    source_ref,
    class_ref,
    count_ref,
    rad,
    rec,
    trans,
    trans_wide,
    table,
    pick_source,
    pick_class,
    kern,
    rays,
    send_out,
    recv_out,
    send_in,
    recv_in,
    small_sem,
    load_sem,
    out_send_sem,
    out_recv_sem,
    in_send_sem,
    in_recv_sem,
):
    n_dev = n_dom * n_tm
    dom, tm = lax.axis_index("dom"), lax.axis_index("tm")
    steps_own, panels = signal_ref.shape
    dirs_all = rad.shape[1]
    classes, lags, _ = trans.shape
    entries, boxes_all = source_ref.shape
    boxes_own = boxes_all // n_dom
    span = LANES // n_tm
    rows_all = n_tm * SUBLANES
    chunks = load_sem.shape[0] - 2
    depth = panels // chunks
    dom_of = flips(dom, n_dom)
    tm_of = flips(tm, n_tm)
    peers = range(n_dev - 1, 0, -1)

    def place(mask):
        return {"dom": dom_of[mask // n_tm], "tm": tm_of[mask % n_tm]}

    def rad_copy(index):
        at = pl.ds(index * depth, depth)
        return pltpu.make_async_copy(rad_hbm.at[at, :], rad.at[at, :], load_sem.at[index])

    rec_copy = pltpu.make_async_copy(rec_hbm, rec, load_sem.at[chunks])
    trans_copy = pltpu.make_async_copy(trans_hbm, trans, load_sem.at[chunks + 1])
    small = [
        pltpu.make_async_copy(source, target, small_sem.at[index])
        for index, (source, target) in enumerate(
            [
                (signal_hbm, signal_ref),
                (box_hbm, box_ref),
                (source_hbm, source_ref),
                (class_hbm, class_ref),
                (count_hbm, count_ref),
            ]
        )
    ]

    barrier = pltpu.get_barrier_semaphore()
    small[0].start()
    small[1].start()
    for index in range(chunks):
        rad_copy(index).start()
    for mask in peers:
        pl.semaphore_signal(barrier, inc=1, device_id=place(mask), device_id_type=MESH)
    trans_copy.start()
    for copy in small[2:]:
        copy.start()
    rec_copy.start()
    small[0].wait()
    small[1].wait()

    lane_group = lax.broadcasted_iota(jnp.int32, (SUBLANES, LANES), 1) // span

    row = lax.broadcasted_iota(jnp.int32, (rows_all, panels), 0)
    row_box = row // (steps_own * SUBLANES) * SUBLANES + row % SUBLANES
    row_step = (row // SUBLANES) % steps_own
    owned = box_ref[...] == row_box
    signal = signal_ref[...].astype(jnp.float32)
    spread = signal[0:1]
    for step in range(1, steps_own):
        spread = jnp.where(row_step == step, signal[step : step + 1], spread)
    masked = jnp.where(owned, spread, 0.0).astype(jnp.bfloat16)

    outgoing = jnp.zeros((rows_all, dirs_all), jnp.float32)
    for index in range(chunks):
        rad_copy(index).wait()
        outgoing = outgoing + jnp.dot(
            masked[:, index * depth : (index + 1) * depth],
            rad[index * depth : (index + 1) * depth, :],
            preferred_element_type=jnp.float32,
        )
    for owner in range(n_dom):
        tiles = [
            outgoing[part * SUBLANES : (part + 1) * SUBLANES, owner * LANES : (owner + 1) * LANES]
            for part in range(n_tm)
        ]
        tiles = swap_groups(tiles, lane_group)
        for time in range(n_tm):
            send_out[dom_of[owner] * n_tm + tm_of[time]] = tiles[time].astype(jnp.bfloat16)

    pl.semaphore_wait(barrier, n_dev - 1)

    def out_copy(mask):
        return pltpu.make_async_remote_copy(
            src_ref=send_out.at[mask],
            dst_ref=recv_out.at[mask],
            send_sem=out_send_sem.at[mask],
            recv_sem=out_recv_sem.at[mask],
            device_id=place(mask),
            device_id_type=MESH,
        )

    def in_copy(mask):
        return pltpu.make_async_remote_copy(
            src_ref=send_in.at[mask],
            dst_ref=recv_in.at[mask],
            send_sem=in_send_sem.at[mask],
            recv_sem=in_recv_sem.at[mask],
            device_id=place(mask),
            device_id_type=MESH,
        )

    for mask in peers:
        out_copy(mask).start()
    recv_out[0] = send_out[0]

    trans_copy.wait()
    trans_wide[...] = trans[...].astype(jnp.float32).reshape(classes * lags, LANES)
    for index in range(classes // (2 * SUBLANES)):
        columns = [[] for _ in range(2 * n_tm)]
        for part in range(2):
            base = (2 * index + part) * SUBLANES * lags
            wide = []
            for lag in range(lags):
                tile = trans_wide[pl.ds(base + lag, SUBLANES, stride=lags), :]
                tile = jnp.where(lane_group == tm, tile, 0.0)
                shift = span
                while shift < LANES:
                    tile = tile + spin(tile, shift)
                    shift *= 2
                wide.append(tile)
            for turn in range(n_tm):
                for half in range(2):
                    tile = jnp.zeros_like(wide[0])
                    for group in range(n_tm):
                        if half == 0 or group <= turn:
                            lag = half * n_tm + (turn - group) % n_tm
                            tile = jnp.where(lane_group == group, wide[lag], tile)
                    columns[2 * turn + half].append(tile)
        at = pl.ds(index * 2 * SUBLANES, 2 * SUBLANES)
        for column, parts in enumerate(columns):
            table[at, column * LANES : (column + 1) * LANES] = jnp.concatenate(
                parts, axis=0
            ).astype(jnp.bfloat16)

    for copy in small[2:]:
        copy.wait()
    used = lax.broadcasted_iota(jnp.int32, class_ref.shape, 0) < count_ref[...]
    kinds = jnp.where(used, class_ref[...], classes).astype(jnp.float32).T
    sources = source_ref[...].astype(jnp.float32).T
    lane = lax.broadcasted_iota(jnp.int32, (boxes_all, LANES), 1).astype(jnp.float32)
    for entry in range(entries):
        pick_class[entry] = jnp.where(
            kinds[:, entry : entry + 1] == lane[:, :classes], 1.0, 0.0
        ).astype(jnp.bfloat16)
        pick_source[entry] = jnp.where(sources[:, entry : entry + 1] == lane, 1.0, 0.0).astype(
            jnp.bfloat16
        )
    for entry in range(entries):
        rows = jnp.dot(pick_class[entry], table[...], preferred_element_type=jnp.float32)
        for column in range(2 * n_tm):
            kern[column, entry * boxes_all : (entry + 1) * boxes_all, :] = rows[
                :, column * LANES : (column + 1) * LANES
            ]

    for mask in range(n_dom):
        tiles = []
        for part in range(n_tm):
            if mask or part:
                out_copy(mask * n_tm + part).wait_recv()
        for time in range(n_tm):
            tiles.append(recv_out[mask * n_tm + tm_of[time]].astype(jnp.float32))
        at = pl.ds(pl.multiple_of(dom_of[mask] * boxes_own, boxes_own), boxes_own)
        low = lane_group < n_tm // 2
        for half in range(2):
            first, second = tiles[2 * half], tiles[2 * half + 1]
            upper = jnp.where(low, first, spin(second, LANES // 2))
            lower = jnp.where(low, spin(first, LANES // 2), second)
            rays[at, half * LANES : (half + 1) * LANES] = jnp.concatenate(
                [upper, lower], axis=0
            ).astype(jnp.bfloat16)

    for mask in range(n_dom - 1, -1, -1):
        first_box = pl.multiple_of(dom_of[mask] * boxes_own, boxes_own)
        picked = jnp.concatenate(
            [pick_source[entry, pl.ds(first_box, boxes_own), :] for entry in range(entries)], axis=0
        )
        found = jnp.dot(picked, rays[...], preferred_element_type=jnp.float32)
        totals = []
        for part in range(2):
            total = [None] * (2 * n_tm)
            for entry in range(entries):
                at = entry * boxes_own + part * SUBLANES
                early = found[at : at + SUBLANES, :LANES]
                late = found[at : at + SUBLANES, LANES:]
                rows = pl.ds(entry * boxes_all + first_box + part * SUBLANES, SUBLANES)
                for turn in range(n_tm):
                    near = kern[2 * turn, rows, :]
                    far = kern[2 * turn + 1, rows, :]
                    if turn == n_tm - 1:
                        young, old = early, late
                    else:
                        young = jnp.where(lane_group <= turn, early, 0.0)
                        old = jnp.where(lane_group <= turn, late, early)
                    adds = [near * young, near * old + far * early]
                    for half in range(2):
                        at_step = half * n_tm + turn
                        total[at_step] = (
                            adds[half] if entry == 0 else total[at_step] + adds[half]
                        )
            totals.append(total)
        for time in range(n_tm):
            sums = [
                totals[part][time * steps_own + step]
                for part in range(2)
                for step in range(steps_own)
            ]
            send_in[mask * n_tm + tm_of[time]] = sum_groups(sums, lane_group).astype(jnp.bfloat16)
        for part in range(n_tm - 1, -1, -1):
            if mask or part:
                in_copy(mask * n_tm + part).start()
    recv_in[0] = send_in[0]

    rec_copy.wait()
    field = jnp.zeros((rows_all, panels), jnp.float32)
    for mask in range(n_dom):
        for part in range(n_tm):
            if mask or part:
                in_copy(mask * n_tm + part).wait_recv()
        tiles = [recv_in[mask * n_tm + tm_of[time]].astype(jnp.float32) for time in range(n_tm)]
        incoming = jnp.concatenate(swap_groups(tiles, lane_group), axis=0).astype(jnp.bfloat16)
        field = field + lax.dot_general(
            incoming,
            rec[:, pl.ds(pl.multiple_of(dom_of[mask] * LANES, LANES), LANES)],
            (((1,), (1,)), ((), ())),
            preferred_element_type=jnp.float32,
        )
    chosen = jnp.where(owned, field, 0.0)
    for step in range(steps_own):
        mine = jnp.where(row_step == step, chosen, 0.0)
        out_ref[step : step + 1, :] = jnp.sum(mine, axis=0, keepdims=True).astype(out_ref.dtype)

    for mask in peers:
        out_copy(mask).wait_send()
        in_copy(mask).wait_send()


def fused_body(
    n_dom,
    n_tm,
    panel_signal,
    panel_box,
    radiation,
    reception,
    translation,
    list_source,
    list_class,
    list_count,
):
    steps_own, panels = panel_signal.shape
    dirs_all = radiation.shape[1]
    classes, lags, _ = translation.shape
    boxes_all, entries = list_source.shape
    n_dev = n_dom * n_tm
    chunks = 4
    vmem = pl.BlockSpec(memory_space=pltpu.VMEM)
    hbm = pl.BlockSpec(memory_space=pl.ANY)
    message = pltpu.VMEM((n_dev, SUBLANES, LANES), jnp.bfloat16)
    lists = pltpu.VMEM((entries, boxes_all), jnp.int32)
    return pl.pallas_call(
        functools.partial(kernel, n_dom, n_tm),
        out_shape=pltpu.VMEM((steps_own, panels), jnp.bfloat16),
        in_specs=[hbm] * 8,
        out_specs=vmem,
        scratch_shapes=[
            pltpu.VMEM((steps_own, panels), jnp.bfloat16),
            pltpu.VMEM((1, panels), jnp.int32),
            lists,
            lists,
            pltpu.VMEM((1, boxes_all), jnp.int32),
            pltpu.VMEM((panels, dirs_all), jnp.bfloat16),
            pltpu.VMEM((panels, dirs_all), jnp.bfloat16),
            pltpu.VMEM(translation.shape, jnp.bfloat16),
            pltpu.VMEM((classes * lags, LANES), jnp.float32),
            pltpu.VMEM((classes, lags * LANES), jnp.bfloat16),
            pltpu.VMEM((entries, boxes_all, boxes_all), jnp.bfloat16),
            pltpu.VMEM((entries, boxes_all, classes), jnp.bfloat16),
            pltpu.VMEM((lags, entries * boxes_all, LANES), jnp.float32),
            pltpu.VMEM((boxes_all, 2 * LANES), jnp.bfloat16),
            message,
            message,
            message,
            message,
            pltpu.SemaphoreType.DMA((5,)),
            pltpu.SemaphoreType.DMA((chunks + 2,)),
            pltpu.SemaphoreType.DMA((n_dev,)),
            pltpu.SemaphoreType.DMA((n_dev,)),
            pltpu.SemaphoreType.DMA((n_dev,)),
            pltpu.SemaphoreType.DMA((n_dev,)),
        ],
        compiler_params=pltpu.CompilerParams(
            collective_id=0, has_side_effects=True
        ),
    )(
        panel_signal,
        panel_box.reshape(1, panels),
        radiation,
        reception,
        translation,
        list_source.T,
        list_class.T,
        list_count.reshape(1, boxes_all),
    )


def whole_body(n_dom, n_tm, *args):
    panel_signal, translation, boxes_all = args[0], args[4], args[5].shape[0]
    steps_own = panel_signal.shape[0]
    classes, lags, dirs_own = translation.shape
    boxes_own = boxes_all // n_dom
    fits = (
        dirs_own == LANES
        and boxes_all == LANES
        and n_dom & (n_dom - 1) == 0
        and n_tm & (n_tm - 1) == 0
        and lags == 2 * n_tm
        and steps_own * n_tm == lags
        and boxes_own == 2 * SUBLANES
        and steps_own * boxes_own == n_tm * SUBLANES
        and classes % (2 * SUBLANES) == 0
        and classes <= LANES
    )
    if fits:
        return fused_body(n_dom, n_tm, *args)
    return body(*args)


def solution(mesh):
    placed = (
        P("tm", "dom"),
        P("dom"),
        P("dom", None),
        P("dom", None),
        P(None, None, "dom"),
        P(),
        P(),
        P(),
    )
    return jax.shard_map(
        functools.partial(whole_body, mesh.shape["dom"], mesh.shape["tm"]),
        mesh=mesh, in_specs=placed, out_specs=P("tm", "dom"), check_vma=False
    )
```

```python
import functools
import math

import jax
import jax.numpy as jnp
from jax import lax
from jax.experimental import pallas as pl
from jax.experimental.pallas import tpu as pltpu
from jax.sharding import PartitionSpec as P

def lag_sum(kern_rows, gathered, out_steps, offset):
    entries = kern_rows.shape[0]
    lags_all = kern_rows.shape[1]
    width = kern_rows.shape[2]
    results = []
    for step_out in range(out_steps):
        total = jnp.zeros((entries, width), jnp.float32)
        for step_in in range(gathered.shape[1]):
            delay = offset + step_out - step_in
            picked = lax.dynamic_index_in_dim(
                kern_rows, jnp.clip(delay, 0, lags_all - 1), 1, keepdims=False
            )
            weight = jnp.where(delay >= 0, picked.astype(jnp.float32), 0.0)
            total = total + weight * gathered[:, step_in].astype(jnp.float32)
        results.append(total)
    return jnp.stack(results, axis=1)


def body(
    panel_signal, panel_box, radiation, reception, translation, list_source, list_class, list_count
):
    rows_own = panel_signal.shape[0]
    dirs_own = translation.shape[2]
    boxes_all = list_source.shape[0]
    classes_all = translation.shape[0]
    lags_all = translation.shape[1]
    BOX_DEV = boxes_all // lax.axis_size("dom")
    J = list_source.shape[1]
    box_onehot = (panel_box[None, :] == jnp.arange(BOX_DEV, dtype=jnp.int32)[:, None]).astype(
        jnp.bfloat16
    )
    used_rows = (jnp.arange(J, dtype=jnp.int32)[None, :] < list_count[:, None]).astype(jnp.bfloat16)
    block_size = math.gcd(boxes_all, 256)

    def translate_all(table, rays, out_steps, offset):
        width = table.shape[2]
        count_in = rays.shape[1]
        flat_table = table.reshape(classes_all, lags_all * width)
        flat_rays = rays.reshape(boxes_all, count_in * width)

        def one_block(index):
            sources = lax.dynamic_slice_in_dim(
                list_source, index * block_size, block_size, 0
            ).reshape(block_size * J)
            classes = lax.dynamic_slice_in_dim(
                list_class, index * block_size, block_size, 0
            ).reshape(block_size * J)
            keep_rows = lax.dynamic_slice_in_dim(
                used_rows, index * block_size, block_size, 0
            ).reshape(block_size * J, 1)
            kern_rows = (jnp.take(flat_table, classes, axis=0) * keep_rows).reshape(
                block_size * J, lags_all, width
            )
            gathered = jnp.take(flat_rays, sources, axis=0).reshape(block_size * J, count_in, width)
            summed = lag_sum(kern_rows, gathered, out_steps, offset)
            return jnp.sum(summed.reshape(block_size, J, out_steps, width), axis=1)

        blocks = lax.map(one_block, jnp.arange(boxes_all // block_size, dtype=jnp.int32))
        return blocks.reshape(boxes_all, out_steps, width)

    masked = panel_signal[:, None, :] * box_onehot[None]
    outgoing = jnp.einsum(
        "rbp,pk->brk", masked, radiation, preferred_element_type=jnp.float32
    ).astype(jnp.bfloat16)
    spread = lax.all_to_all(outgoing, "dom", split_axis=2, concat_axis=0, tiled=True)
    first = lax.axis_index("tm") * rows_own
    empty = jnp.zeros((boxes_all, rows_own, dirs_own), jnp.float32)
    piece = lax.all_gather(spread, "tm", axis=1, tiled=True)

    def active():
        return empty + translate_all(translation, piece, rows_own, first)

    def passive():
        return empty

    incoming = lax.cond(jnp.int32(0) <= first + rows_own - 1, active, passive)
    rays = lax.all_to_all(
        incoming.astype(jnp.bfloat16), "dom", split_axis=0, concat_axis=2, tiled=True
    )
    partial_value = jnp.einsum("brk,pk->brp", rays, reception, preferred_element_type=jnp.float32)
    field = jnp.sum(partial_value * box_onehot.astype(jnp.float32)[:, None, :], axis=0)
    return field.astype(jnp.bfloat16)


LANES = 128
SUBLANES = 8
MESH = pl.DeviceIdType.MESH


def flips(mine, count):
    bits, bit = [], 1
    while bit < count:
        bits.append((bit, lax.rem(lax.div(mine, bit), 2)))
        bit *= 2
    found = []
    for mask in range(count):
        total = jnp.int32(0)
        for bit, value in bits:
            total = total + bit * ((1 - value) if mask & bit else value)
        found.append(total)
    return found


def spin(values, shift):
    shift = shift % LANES
    return values if shift == 0 else pltpu.roll(values, shift, 1)


def swap_groups(tiles, lane_group):
    count = len(tiles)
    span = LANES // count
    tiles = list(tiles)
    width = count // 2
    while width:
        low = (lane_group // width) % 2 == 0
        swapped = list(tiles)
        for index in range(count):
            if (index // width) % 2:
                continue
            first, second = tiles[index], tiles[index + width]
            if width * 2 == count:
                moved = spin(jnp.where(low, second, first), width * span)
                swapped[index] = jnp.where(low, first, moved)
                swapped[index + width] = jnp.where(low, moved, second)
            else:
                swapped[index] = jnp.where(low, first, spin(second, width * span))
                swapped[index + width] = jnp.where(low, spin(first, -width * span), second)
        tiles = swapped
        width //= 2
    return tiles


def sum_groups(sums, lane_group):
    count = len(sums)
    span = LANES // count
    width = count
    while width > 1:
        width //= 2
        low = (lane_group // width) % 2 == 0
        merged = []
        for part in range(width):
            first, second = sums[part], sums[part + width]
            if width * 2 == count:
                moved = spin(jnp.where(low, second, first), width * span)
            else:
                moved = jnp.where(low, spin(first, -width * span), spin(second, width * span))
            merged.append(jnp.where(low, first, second) + moved)
        sums = merged
    return sums[0]


def kernel(
    n_dom,
    n_tm,
    signal_hbm,
    box_hbm,
    rad_hbm,
    rec_hbm,
    trans_hbm,
    source_hbm,
    class_hbm,
    count_hbm,
    out_ref,
    signal_ref,
    box_ref,
    source_ref,
    class_ref,
    count_ref,
    rad,
    rec,
    trans,
    trans_wide,
    table,
    pick_source,
    pick_class,
    kern,
    rays,
    send_out,
    recv_out,
    send_in,
    recv_in,
    small_sem,
    load_sem,
    out_send_sem,
    out_recv_sem,
    in_send_sem,
    in_recv_sem,
):
    n_dev = n_dom * n_tm
    dom, tm = lax.axis_index("dom"), lax.axis_index("tm")
    steps_own, panels = signal_ref.shape
    dirs_all = rad.shape[1]
    classes, lags, _ = trans.shape
    entries, boxes_all = source_ref.shape
    boxes_own = boxes_all // n_dom
    span = LANES // n_tm
    rows_all = n_tm * SUBLANES
    chunks = load_sem.shape[0] - 2
    depth = panels // chunks
    dom_of = flips(dom, n_dom)
    tm_of = flips(tm, n_tm)
    peers = range(n_dev - 1, 0, -1)

    def place(mask):
        return {"dom": dom_of[mask // n_tm], "tm": tm_of[mask % n_tm]}

    def rad_copy(index):
        at = pl.ds(index * depth, depth)
        return pltpu.make_async_copy(rad_hbm.at[at, :], rad.at[at, :], load_sem.at[index])

    rec_copy = pltpu.make_async_copy(rec_hbm, rec, load_sem.at[chunks])
    trans_copy = pltpu.make_async_copy(trans_hbm, trans, load_sem.at[chunks + 1])
    small = [
        pltpu.make_async_copy(source, target, small_sem.at[index])
        for index, (source, target) in enumerate(
            [
                (signal_hbm, signal_ref),
                (box_hbm, box_ref),
                (source_hbm, source_ref),
                (class_hbm, class_ref),
                (count_hbm, count_ref),
            ]
        )
    ]

    barrier = pltpu.get_barrier_semaphore()
    def others(order):
        def run(body):
            for peer_dom, peer_tm in order:
                slot = dom_of[peer_dom] * n_tm + tm_of[peer_tm]

                @pl.when(slot != 0)
                def _():
                    body({"dom": peer_dom, "tm": peer_tm}, slot)

        return run

    bounds = (n_dom // 8, n_dom // 2, n_dom)
    rising = [(peer_dom, peer_tm) for peer_dom in range(n_dom) for peer_tm in range(n_tm)]

    for mask in peers:
        pl.semaphore_signal(barrier, inc=1, device_id=place(mask), device_id_type=MESH)
    small[0].start()
    small[1].start()
    for index in range(chunks):
        rad_copy(index).start()
    trans_copy.start()
    for copy in small[2:]:
        copy.start()
    small[0].wait()
    small[1].wait()

    lane_group = lax.broadcasted_iota(jnp.int32, (SUBLANES, LANES), 1) // span

    row = lax.broadcasted_iota(jnp.int32, (rows_all, panels), 0)
    row_box = row // (steps_own * SUBLANES) * SUBLANES + row % SUBLANES
    row_step = (row // SUBLANES) % steps_own
    owned = box_ref[...] == row_box
    signal = signal_ref[...].astype(jnp.float32)
    spread = signal[0:1]
    for step in range(1, steps_own):
        spread = jnp.where(row_step == step, signal[step : step + 1], spread)
    masked = jnp.where(owned, spread, 0.0).astype(jnp.bfloat16)

    outgoing = jnp.zeros((rows_all, dirs_all), jnp.float32)
    for index in range(chunks):
        rad_copy(index).wait()
        outgoing = outgoing + jnp.dot(
            masked[:, index * depth : (index + 1) * depth],
            rad[index * depth : (index + 1) * depth, :],
            preferred_element_type=jnp.float32,
        )
    for owner in range(n_dom):
        tiles = [
            outgoing[part * SUBLANES : (part + 1) * SUBLANES, owner * LANES : (owner + 1) * LANES]
            for part in range(n_tm)
        ]
        tiles = swap_groups(tiles, lane_group)
        for time in range(n_tm):
            send_out[dom_of[owner] * n_tm + tm_of[time]] = tiles[time].astype(jnp.bfloat16)

    rec_copy.start()
    pl.semaphore_wait(barrier, n_dev - 1)

    def out_copy(slot, peer=None):
        return pltpu.make_async_remote_copy(
            src_ref=send_out.at[slot],
            dst_ref=recv_out.at[slot],
            send_sem=out_send_sem.at[slot],
            recv_sem=out_recv_sem.at[slot],
            device_id=peer or place(slot),
            device_id_type=MESH,
        )

    def in_copy(slot, peer=None):
        return pltpu.make_async_remote_copy(
            src_ref=send_in.at[slot],
            dst_ref=recv_in.at[slot],
            send_sem=in_send_sem.at[slot],
            recv_sem=in_recv_sem.at[slot],
            device_id=peer or place(slot),
            device_id_type=MESH,
        )

    @others(rising[::-1])
    def _(peer, slot):
        out_copy(slot, peer).start()

    recv_out[0] = send_out[0]

    trans_copy.wait()
    trans_wide[...] = trans[...].astype(jnp.float32).reshape(classes * lags, LANES)
    for index in range(classes // (2 * SUBLANES)):
        columns = [[] for _ in range(2 * n_tm)]
        for part in range(2):
            base = (2 * index + part) * SUBLANES * lags
            wide = []
            for lag in range(lags):
                tile = trans_wide[pl.ds(base + lag, SUBLANES, stride=lags), :]
                tile = jnp.where(lane_group == tm, tile, 0.0)
                shift = span
                while shift < LANES:
                    tile = tile + spin(tile, shift)
                    shift *= 2
                wide.append(tile)
            for turn in range(n_tm):
                for half in range(2):
                    tile = jnp.zeros_like(wide[0])
                    for group in range(n_tm):
                        if half == 0 or group <= turn:
                            lag = half * n_tm + (turn - group) % n_tm
                            tile = jnp.where(lane_group == group, wide[lag], tile)
                    columns[2 * turn + half].append(tile)
        at = pl.ds(index * 2 * SUBLANES, 2 * SUBLANES)
        for column, parts in enumerate(columns):
            table[at, column * LANES : (column + 1) * LANES] = jnp.concatenate(
                parts, axis=0
            ).astype(jnp.bfloat16)

    for copy in small[2:]:
        copy.wait()
    used = lax.broadcasted_iota(jnp.int32, class_ref.shape, 0) < count_ref[...]
    kinds = jnp.where(used, class_ref[...], classes).astype(jnp.float32).T
    sources = source_ref[...].astype(jnp.float32).T
    lane = lax.broadcasted_iota(jnp.int32, (boxes_all, LANES), 1).astype(jnp.float32)
    for entry in range(entries):
        pick_class[entry] = jnp.where(
            kinds[:, entry : entry + 1] == lane[:, :classes], 1.0, 0.0
        ).astype(jnp.bfloat16)
        pick_source[entry] = jnp.where(sources[:, entry : entry + 1] == lane, 1.0, 0.0).astype(
            jnp.bfloat16
        )
    for entry in range(entries):
        rows = jnp.dot(pick_class[entry], table[...], preferred_element_type=jnp.float32)
        for column in range(2 * n_tm):
            kern[column, entry * boxes_all : (entry + 1) * boxes_all, :] = rows[
                :, column * LANES : (column + 1) * LANES
            ]

    for mask in range(n_dom):
        tiles = []
        for part in range(n_tm):
            if mask or part:
                out_copy(mask * n_tm + part).wait_recv()
        for time in range(n_tm):
            tiles.append(recv_out[mask * n_tm + tm_of[time]].astype(jnp.float32))
        at = pl.ds(pl.multiple_of(dom_of[mask] * boxes_own, boxes_own), boxes_own)
        low = lane_group < n_tm // 2
        for half in range(2):
            first, second = tiles[2 * half], tiles[2 * half + 1]
            upper = jnp.where(low, first, spin(second, LANES // 2))
            lower = jnp.where(low, spin(first, LANES // 2), second)
            rays[at, half * LANES : (half + 1) * LANES] = jnp.concatenate(
                [upper, lower], axis=0
            ).astype(jnp.bfloat16)

    for owner in range(n_dom):
        first_box = owner * boxes_own
        picked = jnp.concatenate(
            [pick_source[entry, pl.ds(first_box, boxes_own), :] for entry in range(entries)], axis=0
        )
        found = jnp.dot(picked, rays[...], preferred_element_type=jnp.float32)
        totals = []
        for part in range(2):
            total = [None] * (2 * n_tm)
            for entry in range(entries):
                at = entry * boxes_own + part * SUBLANES
                early = found[at : at + SUBLANES, :LANES]
                late = found[at : at + SUBLANES, LANES:]
                rows = pl.ds(entry * boxes_all + first_box + part * SUBLANES, SUBLANES)
                for turn in range(n_tm):
                    near = kern[2 * turn, rows, :]
                    far = kern[2 * turn + 1, rows, :]
                    if turn == n_tm - 1:
                        young, old = early, late
                    else:
                        young = jnp.where(lane_group <= turn, early, 0.0)
                        old = jnp.where(lane_group <= turn, late, early)
                    adds = [near * young, near * old + far * early]
                    for half in range(2):
                        at_step = half * n_tm + turn
                        total[at_step] = (
                            adds[half] if entry == 0 else total[at_step] + adds[half]
                        )
            totals.append(total)
        for time in range(n_tm):
            sums = [
                totals[part][time * steps_own + step]
                for part in range(2)
                for step in range(steps_own)
            ]
            send_in[dom_of[owner] * n_tm + tm_of[time]] = sum_groups(sums, lane_group).astype(jnp.bfloat16)
        if owner + 1 in bounds:
            begin = max([0] + [bound for bound in bounds if bound <= owner])

            @others(rising[begin * n_tm : (owner + 1) * n_tm])
            def _(peer, slot):
                in_copy(slot, peer).start()

    recv_in[0] = send_in[0]

    rec_copy.wait()
    field = jnp.zeros((rows_all, panels), jnp.float32)
    for mask in range(n_dom):
        for part in range(n_tm):
            if mask or part:
                in_copy(mask * n_tm + part).wait_recv()
        tiles = [recv_in[mask * n_tm + tm_of[time]].astype(jnp.float32) for time in range(n_tm)]
        incoming = jnp.concatenate(swap_groups(tiles, lane_group), axis=0).astype(jnp.bfloat16)
        field = field + lax.dot_general(
            incoming,
            rec[:, pl.ds(pl.multiple_of(dom_of[mask] * LANES, LANES), LANES)],
            (((1,), (1,)), ((), ())),
            preferred_element_type=jnp.float32,
        )
    chosen = jnp.where(owned, field, 0.0)
    for step in range(steps_own):
        mine = jnp.where(row_step == step, chosen, 0.0)
        out_ref[step : step + 1, :] = jnp.sum(mine, axis=0, keepdims=True).astype(out_ref.dtype)

    for mask in peers:
        out_copy(mask).wait_send()
        in_copy(mask).wait_send()


def fused_body(
    n_dom,
    n_tm,
    panel_signal,
    panel_box,
    radiation,
    reception,
    translation,
    list_source,
    list_class,
    list_count,
):
    steps_own, panels = panel_signal.shape
    dirs_all = radiation.shape[1]
    classes, lags, _ = translation.shape
    boxes_all, entries = list_source.shape
    n_dev = n_dom * n_tm
    chunks = 4
    vmem = pl.BlockSpec(memory_space=pltpu.VMEM)
    hbm = pl.BlockSpec(memory_space=pl.ANY)
    message = pltpu.VMEM((n_dev, SUBLANES, LANES), jnp.bfloat16)
    lists = pltpu.VMEM((entries, boxes_all), jnp.int32)
    return pl.pallas_call(
        functools.partial(kernel, n_dom, n_tm),
        out_shape=pltpu.VMEM((steps_own, panels), jnp.bfloat16),
        in_specs=[hbm] * 8,
        out_specs=vmem,
        scratch_shapes=[
            pltpu.VMEM((steps_own, panels), jnp.bfloat16),
            pltpu.VMEM((1, panels), jnp.int32),
            lists,
            lists,
            pltpu.VMEM((1, boxes_all), jnp.int32),
            pltpu.VMEM((panels, dirs_all), jnp.bfloat16),
            pltpu.VMEM((panels, dirs_all), jnp.bfloat16),
            pltpu.VMEM(translation.shape, jnp.bfloat16),
            pltpu.VMEM((classes * lags, LANES), jnp.float32),
            pltpu.VMEM((classes, lags * LANES), jnp.bfloat16),
            pltpu.VMEM((entries, boxes_all, boxes_all), jnp.bfloat16),
            pltpu.VMEM((entries, boxes_all, classes), jnp.bfloat16),
            pltpu.VMEM((lags, entries * boxes_all, LANES), jnp.float32),
            pltpu.VMEM((boxes_all, 2 * LANES), jnp.bfloat16),
            message,
            message,
            message,
            message,
            pltpu.SemaphoreType.DMA((5,)),
            pltpu.SemaphoreType.DMA((chunks + 2,)),
            pltpu.SemaphoreType.DMA((n_dev,)),
            pltpu.SemaphoreType.DMA((n_dev,)),
            pltpu.SemaphoreType.DMA((n_dev,)),
            pltpu.SemaphoreType.DMA((n_dev,)),
        ],
        compiler_params=pltpu.CompilerParams(
            collective_id=0, has_side_effects=True
        ),
    )(
        panel_signal,
        panel_box.reshape(1, panels),
        radiation,
        reception,
        translation,
        list_source.T,
        list_class.T,
        list_count.reshape(1, boxes_all),
    )


def whole_body(n_dom, n_tm, *args):
    panel_signal, translation, boxes_all = args[0], args[4], args[5].shape[0]
    steps_own = panel_signal.shape[0]
    classes, lags, dirs_own = translation.shape
    boxes_own = boxes_all // n_dom
    fits = (
        dirs_own == LANES
        and boxes_all == LANES
        and n_dom & (n_dom - 1) == 0
        and n_tm & (n_tm - 1) == 0
        and lags == 2 * n_tm
        and steps_own * n_tm == lags
        and boxes_own == 2 * SUBLANES
        and steps_own * boxes_own == n_tm * SUBLANES
        and classes % (2 * SUBLANES) == 0
        and classes <= LANES
    )
    if fits:
        return fused_body(n_dom, n_tm, *args)
    return body(*args)


def solution(mesh):
    placed = (
        P("tm", "dom"),
        P("dom"),
        P("dom", None),
        P("dom", None),
        P(None, None, "dom"),
        P(),
        P(),
        P(),
    )
    return jax.shard_map(
        functools.partial(whole_body, mesh.shape["dom"], mesh.shape["tm"]),
        mesh=mesh, in_specs=placed, out_specs=P("tm", "dom"), check_vma=False
    )
```

```python
import functools
import math

import jax
import jax.numpy as jnp
from jax import lax
from jax.experimental import pallas as pl
from jax.experimental.pallas import tpu as pltpu
from jax.sharding import PartitionSpec as P

def lag_sum(kern_rows, gathered, out_steps, offset):
    entries = kern_rows.shape[0]
    lags_all = kern_rows.shape[1]
    width = kern_rows.shape[2]
    results = []
    for step_out in range(out_steps):
        total = jnp.zeros((entries, width), jnp.float32)
        for step_in in range(gathered.shape[1]):
            delay = offset + step_out - step_in
            picked = lax.dynamic_index_in_dim(
                kern_rows, jnp.clip(delay, 0, lags_all - 1), 1, keepdims=False
            )
            weight = jnp.where(delay >= 0, picked.astype(jnp.float32), 0.0)
            total = total + weight * gathered[:, step_in].astype(jnp.float32)
        results.append(total)
    return jnp.stack(results, axis=1)


def body(
    panel_signal, panel_box, radiation, reception, translation, list_source, list_class, list_count
):
    rows_own = panel_signal.shape[0]
    dirs_own = translation.shape[2]
    boxes_all = list_source.shape[0]
    classes_all = translation.shape[0]
    lags_all = translation.shape[1]
    BOX_DEV = boxes_all // lax.axis_size("dom")
    J = list_source.shape[1]
    box_onehot = (panel_box[None, :] == jnp.arange(BOX_DEV, dtype=jnp.int32)[:, None]).astype(
        jnp.bfloat16
    )
    used_rows = (jnp.arange(J, dtype=jnp.int32)[None, :] < list_count[:, None]).astype(jnp.bfloat16)
    block_size = math.gcd(boxes_all, 256)

    def translate_all(table, rays, out_steps, offset):
        width = table.shape[2]
        count_in = rays.shape[1]
        flat_table = table.reshape(classes_all, lags_all * width)
        flat_rays = rays.reshape(boxes_all, count_in * width)

        def one_block(index):
            sources = lax.dynamic_slice_in_dim(
                list_source, index * block_size, block_size, 0
            ).reshape(block_size * J)
            classes = lax.dynamic_slice_in_dim(
                list_class, index * block_size, block_size, 0
            ).reshape(block_size * J)
            keep_rows = lax.dynamic_slice_in_dim(
                used_rows, index * block_size, block_size, 0
            ).reshape(block_size * J, 1)
            kern_rows = (jnp.take(flat_table, classes, axis=0) * keep_rows).reshape(
                block_size * J, lags_all, width
            )
            gathered = jnp.take(flat_rays, sources, axis=0).reshape(block_size * J, count_in, width)
            summed = lag_sum(kern_rows, gathered, out_steps, offset)
            return jnp.sum(summed.reshape(block_size, J, out_steps, width), axis=1)

        blocks = lax.map(one_block, jnp.arange(boxes_all // block_size, dtype=jnp.int32))
        return blocks.reshape(boxes_all, out_steps, width)

    masked = panel_signal[:, None, :] * box_onehot[None]
    outgoing = jnp.einsum(
        "rbp,pk->brk", masked, radiation, preferred_element_type=jnp.float32
    ).astype(jnp.bfloat16)
    spread = lax.all_to_all(outgoing, "dom", split_axis=2, concat_axis=0, tiled=True)
    first = lax.axis_index("tm") * rows_own
    empty = jnp.zeros((boxes_all, rows_own, dirs_own), jnp.float32)
    piece = lax.all_gather(spread, "tm", axis=1, tiled=True)

    def active():
        return empty + translate_all(translation, piece, rows_own, first)

    def passive():
        return empty

    incoming = lax.cond(jnp.int32(0) <= first + rows_own - 1, active, passive)
    rays = lax.all_to_all(
        incoming.astype(jnp.bfloat16), "dom", split_axis=0, concat_axis=2, tiled=True
    )
    partial_value = jnp.einsum("brk,pk->brp", rays, reception, preferred_element_type=jnp.float32)
    field = jnp.sum(partial_value * box_onehot.astype(jnp.float32)[:, None, :], axis=0)
    return field.astype(jnp.bfloat16)


LANES = 128
SUBLANES = 8
MESH = pl.DeviceIdType.MESH


def flips(mine, count):
    bits, bit = [], 1
    while bit < count:
        bits.append((bit, lax.rem(lax.div(mine, bit), 2)))
        bit *= 2
    found = []
    for mask in range(count):
        total = jnp.int32(0)
        for bit, value in bits:
            total = total + bit * ((1 - value) if mask & bit else value)
        found.append(total)
    return found


def spin(values, shift):
    shift = shift % LANES
    return values if shift == 0 else pltpu.roll(values, shift, 1)


def swap_groups(tiles, lane_group):
    count = len(tiles)
    span = LANES // count
    tiles = list(tiles)
    width = count // 2
    while width:
        low = (lane_group // width) % 2 == 0
        swapped = list(tiles)
        for index in range(count):
            if (index // width) % 2:
                continue
            first, second = tiles[index], tiles[index + width]
            if width * 2 == count:
                moved = spin(jnp.where(low, second, first), width * span)
                swapped[index] = jnp.where(low, first, moved)
                swapped[index + width] = jnp.where(low, moved, second)
            else:
                swapped[index] = jnp.where(low, first, spin(second, width * span))
                swapped[index + width] = jnp.where(low, spin(first, -width * span), second)
        tiles = swapped
        width //= 2
    return tiles


def sum_groups(sums, lane_group):
    count = len(sums)
    span = LANES // count
    width = count
    while width > 1:
        width //= 2
        low = (lane_group // width) % 2 == 0
        merged = []
        for part in range(width):
            first, second = sums[part], sums[part + width]
            if width * 2 == count:
                moved = spin(jnp.where(low, second, first), width * span)
            else:
                moved = jnp.where(low, spin(first, -width * span), spin(second, width * span))
            merged.append(jnp.where(low, first, second) + moved)
        sums = merged
    return sums[0]


def kernel(
    n_dom,
    n_tm,
    signal_hbm,
    box_hbm,
    rad_hbm,
    rec_hbm,
    trans_hbm,
    source_hbm,
    class_hbm,
    count_hbm,
    out_ref,
    signal_ref,
    box_ref,
    lists_ref,
    count_ref,
    rad,
    rec,
    trans,
    trans_wide,
    table,
    pick_source,
    pick_class,
    kern,
    rays,
    send_out,
    recv_out,
    send_in,
    recv_in,
    small_sem,
    load_sem,
    out_send_sem,
    out_recv_sem,
    in_send_sem,
    in_recv_sem,
):
    n_dev = n_dom * n_tm
    dom, tm = lax.axis_index("dom"), lax.axis_index("tm")
    steps_own, panels = signal_ref.shape
    dirs_all = rad.shape[1]
    classes, lags, _ = trans.shape
    _, entries, boxes_all = lists_ref.shape
    boxes_own = boxes_all // n_dom
    span = LANES // n_tm
    rows_all = n_tm * SUBLANES
    chunks = load_sem.shape[0] - 2
    depth = panels // chunks
    dom_of = flips(dom, n_dom)
    tm_of = flips(tm, n_tm)
    peers = range(n_dev - 1, 0, -1)

    def place(mask):
        return {"dom": dom_of[mask // n_tm], "tm": tm_of[mask % n_tm]}

    def rad_copy(index):
        at = pl.ds(index * depth, depth)
        return pltpu.make_async_copy(rad_hbm.at[at, :], rad.at[at, :], load_sem.at[index])

    rec_copy = pltpu.make_async_copy(rec_hbm, rec, load_sem.at[chunks])
    trans_copy = pltpu.make_async_copy(trans_hbm, trans, load_sem.at[chunks + 1])
    small = [
        pltpu.make_async_copy(signal_hbm, signal_ref, small_sem.at[0]),
        pltpu.make_async_copy(box_hbm, box_ref, small_sem.at[1]),
        pltpu.make_async_copy(count_hbm, count_ref, small_sem.at[2]),
    ]
    lists = [
        pltpu.make_async_copy(source_hbm, lists_ref.at[0], small_sem.at[3]),
        pltpu.make_async_copy(class_hbm, lists_ref.at[1], small_sem.at[3]),
    ]
    lists_both = pltpu.make_async_copy(lists_ref, lists_ref, small_sem.at[3])

    barrier = pltpu.get_barrier_semaphore()
    def others(order):
        def run(body):
            for peer_dom, peer_tm in order:
                slot = dom_of[peer_dom] * n_tm + tm_of[peer_tm]

                @pl.when(slot != 0)
                def _():
                    body({"dom": peer_dom, "tm": peer_tm}, slot, dom_of[peer_dom])

        return run

    bounds = (n_dom // 8, n_dom // 2, n_dom)
    rising = [(peer_dom, peer_tm) for peer_dom in range(n_dom) for peer_tm in range(n_tm)]

    for mask in peers:
        pl.semaphore_signal(barrier, inc=1, device_id=place(mask), device_id_type=MESH)
    small[0].start()
    small[1].start()
    for index in range(chunks):
        rad_copy(index).start()
    trans_copy.start()
    for copy in [small[2]] + lists:
        copy.start()
    small[0].wait()
    small[1].wait()

    lane_group = lax.broadcasted_iota(jnp.int32, (SUBLANES, LANES), 1) // span

    row = lax.broadcasted_iota(jnp.int32, (rows_all, panels), 0)
    row_box = row // (steps_own * SUBLANES) * SUBLANES + row % SUBLANES
    row_step = (row // SUBLANES) % steps_own
    owned = box_ref[...] == row_box
    signal = signal_ref[...].astype(jnp.float32)
    spread = signal[0:1]
    for step in range(1, steps_own):
        spread = jnp.where(row_step == step, signal[step : step + 1], spread)
    masked = jnp.where(owned, spread, 0.0).astype(jnp.bfloat16)

    outgoing = jnp.zeros((rows_all, dirs_all), jnp.float32)
    for index in range(chunks):
        rad_copy(index).wait()
        outgoing = outgoing + jnp.dot(
            masked[:, index * depth : (index + 1) * depth],
            rad[index * depth : (index + 1) * depth, :],
            preferred_element_type=jnp.float32,
        )
    for owner in range(n_dom):
        tiles = [
            outgoing[part * SUBLANES : (part + 1) * SUBLANES, owner * LANES : (owner + 1) * LANES]
            for part in range(n_tm)
        ]
        tiles = swap_groups(tiles, lane_group)
        for time in range(n_tm):
            send_out[dom_of[owner] * n_tm + tm_of[time]] = tiles[time].astype(jnp.bfloat16)

    rec_copy.start()
    pl.semaphore_wait(barrier, n_dev - 1)

    def exchange(source, target, send_sem, recv_sem):
        def copy(at, peer, group):
            return pltpu.make_async_remote_copy(
                src_ref=source.at[at],
                dst_ref=target.at[at],
                send_sem=send_sem.at[0],
                recv_sem=recv_sem.at[group],
                device_id=peer,
                device_id_type=MESH,
            )

        size = n_dev // recv_sem.shape[0]

        def start(peer, slot, slot_dom):
            copy(slot, peer, lax.div(slot_dom * n_tm, size)).start()

        def take(group):
            first = max(1, group * size)
            copy(pl.ds(first, (group + 1) * size - first), place(first), group).wait_recv()

        def drain():
            copy(pl.ds(1, n_dev - 1), place(1), 0).wait_send()

        return start, take, drain

    out_start, out_take, out_drain = exchange(send_out, recv_out, out_send_sem, out_recv_sem)
    in_start, in_take, in_drain = exchange(send_in, recv_in, in_send_sem, in_recv_sem)

    @others(rising[::-1])
    def _(*where):
        out_start(*where)

    recv_out[0] = send_out[0]

    trans_copy.wait()
    trans_wide[...] = trans[...].astype(jnp.float32).reshape(classes * lags, LANES)
    for index in range(classes // (2 * SUBLANES)):
        columns = [[] for _ in range(2 * n_tm)]
        for part in range(2):
            base = (2 * index + part) * SUBLANES * lags
            wide = []
            for lag in range(lags):
                tile = trans_wide[pl.ds(base + lag, SUBLANES, stride=lags), :]
                tile = jnp.where(lane_group == tm, tile, 0.0)
                shift = span
                while shift < LANES:
                    tile = tile + spin(tile, shift)
                    shift *= 2
                wide.append(tile)
            for turn in range(n_tm):
                for half in range(2):
                    tile = jnp.zeros_like(wide[0])
                    for group in range(n_tm):
                        if half == 0 or group <= turn:
                            lag = half * n_tm + (turn - group) % n_tm
                            tile = jnp.where(lane_group == group, wide[lag], tile)
                    columns[2 * turn + half].append(tile)
        at = pl.ds(index * 2 * SUBLANES, 2 * SUBLANES)
        for column, parts in enumerate(columns):
            table[at, column * LANES : (column + 1) * LANES] = jnp.concatenate(
                parts, axis=0
            ).astype(jnp.bfloat16)

    small[2].wait()
    lists_both.wait()
    used = lax.broadcasted_iota(jnp.int32, (entries, boxes_all), 0) < count_ref[...]
    kinds = jnp.where(used, lists_ref[1], classes).astype(jnp.float32).T
    sources = lists_ref[0].astype(jnp.float32).T
    lane = lax.broadcasted_iota(jnp.int32, (boxes_all, LANES), 1).astype(jnp.float32)
    for entry in range(entries):
        pick_class[entry] = jnp.where(
            kinds[:, entry : entry + 1] == lane[:, :classes], 1.0, 0.0
        ).astype(jnp.bfloat16)
        pick_source[entry] = jnp.where(sources[:, entry : entry + 1] == lane, 1.0, 0.0).astype(
            jnp.bfloat16
        )
    for entry in range(entries):
        rows = jnp.dot(pick_class[entry], table[...], preferred_element_type=jnp.float32)
        for column in range(2 * n_tm):
            kern[column, entry * boxes_all : (entry + 1) * boxes_all, :] = rows[
                :, column * LANES : (column + 1) * LANES
            ]

    for mask in range(n_dom):
        tiles = []
        if mask % (n_dom // out_recv_sem.shape[0]) == 0:
            out_take(mask // (n_dom // out_recv_sem.shape[0]))
        for time in range(n_tm):
            tiles.append(recv_out[mask * n_tm + tm_of[time]].astype(jnp.float32))
        at = pl.ds(pl.multiple_of(dom_of[mask] * boxes_own, boxes_own), boxes_own)
        low = lane_group < n_tm // 2
        for half in range(2):
            first, second = tiles[2 * half], tiles[2 * half + 1]
            upper = jnp.where(low, first, spin(second, LANES // 2))
            lower = jnp.where(low, spin(first, LANES // 2), second)
            rays[at, half * LANES : (half + 1) * LANES] = jnp.concatenate(
                [upper, lower], axis=0
            ).astype(jnp.bfloat16)

    for owner in range(n_dom):
        first_box = owner * boxes_own
        picked = jnp.concatenate(
            [pick_source[entry, pl.ds(first_box, boxes_own), :] for entry in range(entries)], axis=0
        )
        found = jnp.dot(picked, rays[...], preferred_element_type=jnp.float32)
        totals = []
        for part in range(2):
            total = [None] * (2 * n_tm)
            for entry in range(entries):
                at = entry * boxes_own + part * SUBLANES
                early = found[at : at + SUBLANES, :LANES]
                late = found[at : at + SUBLANES, LANES:]
                rows = pl.ds(entry * boxes_all + first_box + part * SUBLANES, SUBLANES)
                for turn in range(n_tm):
                    near = kern[2 * turn, rows, :]
                    far = kern[2 * turn + 1, rows, :]
                    if turn == n_tm - 1:
                        young, old = early, late
                    else:
                        young = jnp.where(lane_group <= turn, early, 0.0)
                        old = jnp.where(lane_group <= turn, late, early)
                    adds = [near * young, near * old + far * early]
                    for half in range(2):
                        at_step = half * n_tm + turn
                        total[at_step] = (
                            adds[half] if entry == 0 else total[at_step] + adds[half]
                        )
            totals.append(total)
        for time in range(n_tm):
            sums = [
                totals[part][time * steps_own + step]
                for part in range(2)
                for step in range(steps_own)
            ]
            send_in[dom_of[owner] * n_tm + tm_of[time]] = sum_groups(sums, lane_group).astype(jnp.bfloat16)
        if owner + 1 in bounds:
            begin = max([0] + [bound for bound in bounds if bound <= owner])

            @others(rising[begin * n_tm : (owner + 1) * n_tm])
            def _(*where):
                in_start(*where)

    recv_in[0] = send_in[0]

    out_drain()
    rec_copy.wait()
    field = jnp.zeros((rows_all, panels), jnp.float32)
    for mask in range(n_dom):
        if mask == n_dom // 2:
            in_drain()
        if mask % (n_dom // in_recv_sem.shape[0]) == 0:
            in_take(mask // (n_dom // in_recv_sem.shape[0]))
        tiles = [recv_in[mask * n_tm + tm_of[time]].astype(jnp.float32) for time in range(n_tm)]
        incoming = jnp.concatenate(swap_groups(tiles, lane_group), axis=0).astype(jnp.bfloat16)
        field = field + lax.dot_general(
            incoming,
            rec[:, pl.ds(pl.multiple_of(dom_of[mask] * LANES, LANES), LANES)],
            (((1,), (1,)), ((), ())),
            preferred_element_type=jnp.float32,
        )
    chosen = jnp.where(owned, field, 0.0)
    for step in range(steps_own):
        mine = jnp.where(row_step == step, chosen, 0.0)
        out_ref[step : step + 1, :] = jnp.sum(mine, axis=0, keepdims=True).astype(out_ref.dtype)


def fused_body(
    n_dom,
    n_tm,
    panel_signal,
    panel_box,
    radiation,
    reception,
    translation,
    list_source,
    list_class,
    list_count,
):
    steps_own, panels = panel_signal.shape
    dirs_all = radiation.shape[1]
    classes, lags, _ = translation.shape
    boxes_all, entries = list_source.shape
    n_dev = n_dom * n_tm
    chunks = 4
    vmem = pl.BlockSpec(memory_space=pltpu.VMEM)
    hbm = pl.BlockSpec(memory_space=pl.ANY)
    message = pltpu.VMEM((n_dev, SUBLANES, LANES), jnp.bfloat16)
    return pl.pallas_call(
        functools.partial(kernel, n_dom, n_tm),
        out_shape=pltpu.VMEM((steps_own, panels), jnp.bfloat16),
        in_specs=[hbm] * 8,
        out_specs=vmem,
        scratch_shapes=[
            pltpu.VMEM((steps_own, panels), jnp.bfloat16),
            pltpu.VMEM((1, panels), jnp.int32),
            pltpu.VMEM((2, entries, boxes_all), jnp.int32),
            pltpu.VMEM((1, boxes_all), jnp.int32),
            pltpu.VMEM((panels, dirs_all), jnp.bfloat16),
            pltpu.VMEM((panels, dirs_all), jnp.bfloat16),
            pltpu.VMEM(translation.shape, jnp.bfloat16),
            pltpu.VMEM((classes * lags, LANES), jnp.float32),
            pltpu.VMEM((classes, lags * LANES), jnp.bfloat16),
            pltpu.VMEM((entries, boxes_all, boxes_all), jnp.bfloat16),
            pltpu.VMEM((entries, boxes_all, classes), jnp.bfloat16),
            pltpu.VMEM((lags, entries * boxes_all, LANES), jnp.float32),
            pltpu.VMEM((boxes_all, 2 * LANES), jnp.bfloat16),
            message,
            message,
            message,
            message,
            pltpu.SemaphoreType.DMA((4,)),
            pltpu.SemaphoreType.DMA((chunks + 2,)),
            pltpu.SemaphoreType.DMA((1,)),
            pltpu.SemaphoreType.DMA((2,)),
            pltpu.SemaphoreType.DMA((1,)),
            pltpu.SemaphoreType.DMA((4,)),
        ],
        compiler_params=pltpu.CompilerParams(
            collective_id=0, has_side_effects=True
        ),
    )(
        panel_signal,
        panel_box.reshape(1, panels),
        radiation,
        reception,
        translation,
        list_source.T,
        list_class.T,
        list_count.reshape(1, boxes_all),
    )


def whole_body(n_dom, n_tm, *args):
    panel_signal, translation, boxes_all = args[0], args[4], args[5].shape[0]
    steps_own = panel_signal.shape[0]
    classes, lags, dirs_own = translation.shape
    boxes_own = boxes_all // n_dom
    fits = (
        dirs_own == LANES
        and boxes_all == LANES
        and n_dom & (n_dom - 1) == 0
        and n_tm & (n_tm - 1) == 0
        and lags == 2 * n_tm
        and steps_own * n_tm == lags
        and boxes_own == 2 * SUBLANES
        and steps_own * boxes_own == n_tm * SUBLANES
        and classes % (2 * SUBLANES) == 0
        and classes <= LANES
    )
    if fits:
        return fused_body(n_dom, n_tm, *args)
    return body(*args)


def solution(mesh):
    placed = (
        P("tm", "dom"),
        P("dom"),
        P("dom", None),
        P("dom", None),
        P(None, None, "dom"),
        P(),
        P(),
        P(),
    )
    return jax.shard_map(
        functools.partial(whole_body, mesh.shape["dom"], mesh.shape["tm"]),
        mesh=mesh, in_specs=placed, out_specs=P("tm", "dom"), check_vma=False
    )
```

```python
import functools
import math

import jax
import jax.numpy as jnp
from jax import lax
from jax.experimental import pallas as pl
from jax.experimental.pallas import tpu as pltpu
from jax.sharding import PartitionSpec as P

def lag_sum(kern_rows, gathered, out_steps, offset):
    entries = kern_rows.shape[0]
    lags_all = kern_rows.shape[1]
    width = kern_rows.shape[2]
    results = []
    for step_out in range(out_steps):
        total = jnp.zeros((entries, width), jnp.float32)
        for step_in in range(gathered.shape[1]):
            delay = offset + step_out - step_in
            picked = lax.dynamic_index_in_dim(
                kern_rows, jnp.clip(delay, 0, lags_all - 1), 1, keepdims=False
            )
            weight = jnp.where(delay >= 0, picked.astype(jnp.float32), 0.0)
            total = total + weight * gathered[:, step_in].astype(jnp.float32)
        results.append(total)
    return jnp.stack(results, axis=1)


def body(
    panel_signal, panel_box, radiation, reception, translation, list_source, list_class, list_count
):
    rows_own = panel_signal.shape[0]
    dirs_own = translation.shape[2]
    boxes_all = list_source.shape[0]
    classes_all = translation.shape[0]
    lags_all = translation.shape[1]
    BOX_DEV = boxes_all // lax.axis_size("dom")
    J = list_source.shape[1]
    box_onehot = (panel_box[None, :] == jnp.arange(BOX_DEV, dtype=jnp.int32)[:, None]).astype(
        jnp.bfloat16
    )
    used_rows = (jnp.arange(J, dtype=jnp.int32)[None, :] < list_count[:, None]).astype(jnp.bfloat16)
    block_size = math.gcd(boxes_all, 256)

    def translate_all(table, rays, out_steps, offset):
        width = table.shape[2]
        count_in = rays.shape[1]
        flat_table = table.reshape(classes_all, lags_all * width)
        flat_rays = rays.reshape(boxes_all, count_in * width)

        def one_block(index):
            sources = lax.dynamic_slice_in_dim(
                list_source, index * block_size, block_size, 0
            ).reshape(block_size * J)
            classes = lax.dynamic_slice_in_dim(
                list_class, index * block_size, block_size, 0
            ).reshape(block_size * J)
            keep_rows = lax.dynamic_slice_in_dim(
                used_rows, index * block_size, block_size, 0
            ).reshape(block_size * J, 1)
            kern_rows = (jnp.take(flat_table, classes, axis=0) * keep_rows).reshape(
                block_size * J, lags_all, width
            )
            gathered = jnp.take(flat_rays, sources, axis=0).reshape(block_size * J, count_in, width)
            summed = lag_sum(kern_rows, gathered, out_steps, offset)
            return jnp.sum(summed.reshape(block_size, J, out_steps, width), axis=1)

        blocks = lax.map(one_block, jnp.arange(boxes_all // block_size, dtype=jnp.int32))
        return blocks.reshape(boxes_all, out_steps, width)

    masked = panel_signal[:, None, :] * box_onehot[None]
    outgoing = jnp.einsum(
        "rbp,pk->brk", masked, radiation, preferred_element_type=jnp.float32
    ).astype(jnp.bfloat16)
    spread = lax.all_to_all(outgoing, "dom", split_axis=2, concat_axis=0, tiled=True)
    first = lax.axis_index("tm") * rows_own
    empty = jnp.zeros((boxes_all, rows_own, dirs_own), jnp.float32)
    piece = lax.all_gather(spread, "tm", axis=1, tiled=True)

    def active():
        return empty + translate_all(translation, piece, rows_own, first)

    def passive():
        return empty

    incoming = lax.cond(jnp.int32(0) <= first + rows_own - 1, active, passive)
    rays = lax.all_to_all(
        incoming.astype(jnp.bfloat16), "dom", split_axis=0, concat_axis=2, tiled=True
    )
    partial_value = jnp.einsum("brk,pk->brp", rays, reception, preferred_element_type=jnp.float32)
    field = jnp.sum(partial_value * box_onehot.astype(jnp.float32)[:, None, :], axis=0)
    return field.astype(jnp.bfloat16)


LANES = 128
SUBLANES = 8
MESH = pl.DeviceIdType.MESH


def flips(mine, count):
    bits, bit = [], 1
    while bit < count:
        bits.append((bit, lax.rem(lax.div(mine, bit), 2)))
        bit *= 2
    found = []
    for mask in range(count):
        total = jnp.int32(0)
        for bit, value in bits:
            total = total + bit * ((1 - value) if mask & bit else value)
        found.append(total)
    return found


def spin(values, shift):
    shift = shift % LANES
    return values if shift == 0 else pltpu.roll(values, shift, 1)


def swap_groups(tiles, lane_group):
    count = len(tiles)
    span = LANES // count
    tiles = list(tiles)
    width = count // 2
    while width:
        low = (lane_group // width) % 2 == 0
        swapped = list(tiles)
        for index in range(count):
            if (index // width) % 2:
                continue
            first, second = tiles[index], tiles[index + width]
            if width * 2 == count:
                moved = spin(jnp.where(low, second, first), width * span)
                swapped[index] = jnp.where(low, first, moved)
                swapped[index + width] = jnp.where(low, moved, second)
            else:
                swapped[index] = jnp.where(low, first, spin(second, width * span))
                swapped[index + width] = jnp.where(low, spin(first, -width * span), second)
        tiles = swapped
        width //= 2
    return tiles


def sum_groups(sums, lane_group):
    count = len(sums)
    span = LANES // count
    width = count
    while width > 1:
        width //= 2
        low = (lane_group // width) % 2 == 0
        merged = []
        for part in range(width):
            first, second = sums[part], sums[part + width]
            if width * 2 == count:
                moved = spin(jnp.where(low, second, first), width * span)
            else:
                moved = jnp.where(low, spin(first, -width * span), spin(second, width * span))
            merged.append(jnp.where(low, first, second) + moved)
        sums = merged
    return sums[0]


def kernel(
    n_dom,
    n_tm,
    signal_hbm,
    box_hbm,
    rad_hbm,
    rec_hbm,
    trans_hbm,
    source_hbm,
    class_hbm,
    count_hbm,
    out_ref,
    signal_ref,
    box_ref,
    lists_ref,
    count_ref,
    rad,
    rec,
    trans,
    trans_wide,
    table,
    pick_source,
    pick_class,
    kern,
    rays,
    send_out,
    recv_out,
    send_in,
    recv_in,
    small_sem,
    load_sem,
    out_send_sem,
    out_recv_sem,
    in_send_sem,
    in_recv_sem,
):
    n_dev = n_dom * n_tm
    dom, tm = lax.axis_index("dom"), lax.axis_index("tm")
    steps_own, panels = signal_ref.shape
    dirs_all = rad.shape[1]
    classes, lags, _ = trans.shape
    _, entries, boxes_all = lists_ref.shape
    boxes_own = boxes_all // n_dom
    span = LANES // n_tm
    rows_all = n_tm * SUBLANES
    chunks = load_sem.shape[0] - 2
    depth = panels // chunks
    dom_of = flips(dom, n_dom)
    tm_of = flips(tm, n_tm)
    peers = range(n_dev - 1, 0, -1)

    def place(mask):
        return {"dom": dom_of[mask // n_tm], "tm": tm_of[mask % n_tm]}

    def rad_copy(index):
        at = pl.ds(index * depth, depth)
        return pltpu.make_async_copy(rad_hbm.at[at, :], rad.at[at, :], load_sem.at[index])

    rec_copy = pltpu.make_async_copy(rec_hbm, rec, load_sem.at[chunks])
    trans_copy = pltpu.make_async_copy(trans_hbm, trans, load_sem.at[chunks + 1])
    small = [
        pltpu.make_async_copy(signal_hbm, signal_ref, small_sem.at[0]),
        pltpu.make_async_copy(box_hbm, box_ref, small_sem.at[1]),
        pltpu.make_async_copy(count_hbm, count_ref, small_sem.at[2]),
    ]
    lists = [
        pltpu.make_async_copy(source_hbm, lists_ref.at[0], small_sem.at[3]),
        pltpu.make_async_copy(class_hbm, lists_ref.at[1], small_sem.at[3]),
    ]
    lists_both = pltpu.make_async_copy(lists_ref, lists_ref, small_sem.at[3])

    barrier = pltpu.get_barrier_semaphore()
    def others(order):
        def run(body):
            for peer_dom, peer_tm in order:
                slot = dom_of[peer_dom] * n_tm + tm_of[peer_tm]

                @pl.when(slot != 0)
                def _():
                    body({"dom": peer_dom, "tm": peer_tm}, slot, dom_of[peer_dom])

        return run

    bounds = (n_tm // 2, n_dev // 2, n_dev)
    rising = [(peer_dom, peer_tm) for peer_dom in range(n_dom) for peer_tm in range(n_tm)]

    for mask in peers:
        pl.semaphore_signal(barrier, inc=1, device_id=place(mask), device_id_type=MESH)
    small[0].start()
    small[1].start()
    for index in range(chunks):
        rad_copy(index).start()
    trans_copy.start()
    for copy in [small[2]] + lists:
        copy.start()
    small[0].wait()
    small[1].wait()

    lane_group = lax.broadcasted_iota(jnp.int32, (SUBLANES, LANES), 1) // span

    row = lax.broadcasted_iota(jnp.int32, (rows_all, panels), 0)
    row_box = row // (steps_own * SUBLANES) * SUBLANES + row % SUBLANES
    row_step = (row // SUBLANES) % steps_own
    owned = box_ref[...] == row_box
    signal = signal_ref[...].astype(jnp.float32)
    spread = signal[0:1]
    for step in range(1, steps_own):
        spread = jnp.where(row_step == step, signal[step : step + 1], spread)
    masked = jnp.where(owned, spread, 0.0).astype(jnp.bfloat16)

    outgoing = jnp.zeros((rows_all, dirs_all), jnp.float32)
    for index in range(chunks):
        rad_copy(index).wait()
        outgoing = outgoing + jnp.dot(
            masked[:, index * depth : (index + 1) * depth],
            rad[index * depth : (index + 1) * depth, :],
            preferred_element_type=jnp.float32,
        )
    for owner in range(n_dom):
        tiles = [
            outgoing[part * SUBLANES : (part + 1) * SUBLANES, owner * LANES : (owner + 1) * LANES]
            for part in range(n_tm)
        ]
        tiles = swap_groups(tiles, lane_group)
        for time in range(n_tm):
            send_out[dom_of[owner] * n_tm + tm_of[time]] = tiles[time].astype(jnp.bfloat16)

    rec_copy.start()
    pl.semaphore_wait(barrier, n_dev - 1)

    def exchange(source, target, send_sem, recv_sem):
        def copy(at, peer, group):
            return pltpu.make_async_remote_copy(
                src_ref=source.at[at],
                dst_ref=target.at[at],
                send_sem=send_sem.at[0],
                recv_sem=recv_sem.at[group],
                device_id=peer,
                device_id_type=MESH,
            )

        size = n_dev // recv_sem.shape[0]

        def start(peer, slot, slot_dom):
            copy(slot, peer, lax.div(slot_dom * n_tm, size)).start()

        def take(group):
            first = max(1, group * size)
            copy(pl.ds(first, (group + 1) * size - first), place(first), group).wait_recv()

        def drain():
            copy(pl.ds(1, n_dev - 1), place(1), 0).wait_send()

        return start, take, drain

    out_start, out_take, out_drain = exchange(send_out, recv_out, out_send_sem, out_recv_sem)
    in_start, in_take, in_drain = exchange(send_in, recv_in, in_send_sem, in_recv_sem)

    @others(sorted(rising, key=lambda at: (-at[0], at[1] % 2, -at[1])))
    def _(*where):
        out_start(*where)

    recv_out[0] = send_out[0]

    trans_copy.wait()
    trans_wide[...] = trans[...].astype(jnp.float32).reshape(classes * lags, LANES)
    for index in range(classes // (2 * SUBLANES)):
        columns = [[] for _ in range(2 * n_tm)]
        for part in range(2):
            base = (2 * index + part) * SUBLANES * lags
            wide = []
            for lag in range(lags):
                tile = trans_wide[pl.ds(base + lag, SUBLANES, stride=lags), :]
                tile = jnp.where(lane_group == tm, tile, 0.0)
                shift = span
                while shift < LANES:
                    tile = tile + spin(tile, shift)
                    shift *= 2
                wide.append(tile)
            for turn in range(n_tm):
                for half in range(2):
                    tile = jnp.zeros_like(wide[0])
                    for group in range(n_tm):
                        if half == 0 or group <= turn:
                            lag = half * n_tm + (turn - group) % n_tm
                            tile = jnp.where(lane_group == group, wide[lag], tile)
                    columns[2 * turn + half].append(tile)
        at = pl.ds(index * 2 * SUBLANES, 2 * SUBLANES)
        for column, parts in enumerate(columns):
            table[at, column * LANES : (column + 1) * LANES] = jnp.concatenate(
                parts, axis=0
            ).astype(jnp.bfloat16)

    small[2].wait()
    lists_both.wait()
    used = lax.broadcasted_iota(jnp.int32, (entries, boxes_all), 0) < count_ref[...]
    kinds = jnp.where(used, lists_ref[1], classes).astype(jnp.float32).T
    sources = lists_ref[0].astype(jnp.float32).T
    lane = lax.broadcasted_iota(jnp.int32, (boxes_all, LANES), 1).astype(jnp.float32)
    for entry in range(entries):
        pick_class[entry] = jnp.where(
            kinds[:, entry : entry + 1] == lane[:, :classes], 1.0, 0.0
        ).astype(jnp.bfloat16)
        pick_source[entry] = jnp.where(sources[:, entry : entry + 1] == lane, 1.0, 0.0).astype(
            jnp.bfloat16
        )
    for entry in range(entries):
        rows = jnp.dot(pick_class[entry], table[...], preferred_element_type=jnp.float32)
        for column in range(2 * n_tm):
            kern[column, entry * boxes_all : (entry + 1) * boxes_all, :] = rows[
                :, column * LANES : (column + 1) * LANES
            ]

    for mask in range(n_dom):
        tiles = []
        if mask % (n_dom // out_recv_sem.shape[0]) == 0:
            out_take(mask // (n_dom // out_recv_sem.shape[0]))
        for time in range(n_tm):
            tiles.append(recv_out[mask * n_tm + tm_of[time]].astype(jnp.float32))
        at = pl.ds(pl.multiple_of(dom_of[mask] * boxes_own, boxes_own), boxes_own)
        low = lane_group < n_tm // 2
        for half in range(2):
            first, second = tiles[2 * half], tiles[2 * half + 1]
            upper = jnp.where(low, first, spin(second, LANES // 2))
            lower = jnp.where(low, spin(first, LANES // 2), second)
            rays[at, half * LANES : (half + 1) * LANES] = jnp.concatenate(
                [upper, lower], axis=0
            ).astype(jnp.bfloat16)

    times = n_tm // 2

    def translate(owner, half):
        first_box = owner * boxes_own
        picked = jnp.concatenate(
            [pick_source[entry, pl.ds(first_box, boxes_own), :] for entry in range(entries)], axis=0
        )
        found = jnp.dot(
            picked, rays[:, : (half + 1) * LANES], preferred_element_type=jnp.float32
        )
        totals = []
        for part in range(2):
            total = [None] * n_tm
            for entry in range(entries):
                at = entry * boxes_own + part * SUBLANES
                early = found[at : at + SUBLANES, :LANES]
                rows = pl.ds(entry * boxes_all + first_box + part * SUBLANES, SUBLANES)
                for turn in range(n_tm):
                    add = kern[2 * turn, rows, :]
                    if half == 0:
                        if turn < n_tm - 1:
                            add = add * jnp.where(lane_group <= turn, early, 0.0)
                        else:
                            add = add * early
                    else:
                        late = found[at : at + SUBLANES, LANES:]
                        if turn < n_tm - 1:
                            late = jnp.where(lane_group <= turn, late, early)
                        add = add * late + kern[2 * turn + 1, rows, :] * early
                    total[turn] = add if entry == 0 else total[turn] + add
            totals.append(total)
        for time in range(times):
            sums = [
                totals[part][time * steps_own + step]
                for part in range(2)
                for step in range(steps_own)
            ]
            send_in[dom_of[owner] * n_tm + tm_of[half * times + time]] = sum_groups(
                sums, lane_group
            ).astype(jnp.bfloat16)

    begin = 0
    for owner in range(n_dom):
        for half in range(2):
            translate(owner, half)
            end = owner * n_tm + (half + 1) * times
            if end not in bounds:
                continue

            @others(rising[begin:end])
            def _(*where):
                in_start(*where)

            begin = end

    recv_in[0] = send_in[0]

    out_drain()
    rec_copy.wait()
    field = jnp.zeros((rows_all, panels), jnp.float32)
    for mask in range(n_dom):
        if mask == n_dom // 2:
            in_drain()
        if mask % (n_dom // in_recv_sem.shape[0]) == 0:
            in_take(mask // (n_dom // in_recv_sem.shape[0]))
        tiles = [recv_in[mask * n_tm + tm_of[time]].astype(jnp.float32) for time in range(n_tm)]
        incoming = jnp.concatenate(swap_groups(tiles, lane_group), axis=0).astype(jnp.bfloat16)
        field = field + lax.dot_general(
            incoming,
            rec[:, pl.ds(pl.multiple_of(dom_of[mask] * LANES, LANES), LANES)],
            (((1,), (1,)), ((), ())),
            preferred_element_type=jnp.float32,
        )
    chosen = jnp.where(owned, field, 0.0)
    for step in range(steps_own):
        mine = jnp.where(row_step == step, chosen, 0.0)
        out_ref[step : step + 1, :] = jnp.sum(mine, axis=0, keepdims=True).astype(out_ref.dtype)


def fused_body(
    n_dom,
    n_tm,
    panel_signal,
    panel_box,
    radiation,
    reception,
    translation,
    list_source,
    list_class,
    list_count,
):
    steps_own, panels = panel_signal.shape
    dirs_all = radiation.shape[1]
    classes, lags, _ = translation.shape
    boxes_all, entries = list_source.shape
    n_dev = n_dom * n_tm
    chunks = 2
    vmem = pl.BlockSpec(memory_space=pltpu.VMEM)
    hbm = pl.BlockSpec(memory_space=pl.ANY)
    message = pltpu.VMEM((n_dev, SUBLANES, LANES), jnp.bfloat16)
    return pl.pallas_call(
        functools.partial(kernel, n_dom, n_tm),
        out_shape=pltpu.VMEM((steps_own, panels), jnp.bfloat16),
        in_specs=[hbm] * 8,
        out_specs=vmem,
        scratch_shapes=[
            pltpu.VMEM((steps_own, panels), jnp.bfloat16),
            pltpu.VMEM((1, panels), jnp.int32),
            pltpu.VMEM((2, entries, boxes_all), jnp.int32),
            pltpu.VMEM((1, boxes_all), jnp.int32),
            pltpu.VMEM((panels, dirs_all), jnp.bfloat16),
            pltpu.VMEM((panels, dirs_all), jnp.bfloat16),
            pltpu.VMEM(translation.shape, jnp.bfloat16),
            pltpu.VMEM((classes * lags, LANES), jnp.float32),
            pltpu.VMEM((classes, lags * LANES), jnp.bfloat16),
            pltpu.VMEM((entries, boxes_all, boxes_all), jnp.bfloat16),
            pltpu.VMEM((entries, boxes_all, classes), jnp.bfloat16),
            pltpu.VMEM((lags, entries * boxes_all, LANES), jnp.float32),
            pltpu.VMEM((boxes_all, 2 * LANES), jnp.bfloat16),
            message,
            message,
            message,
            message,
            pltpu.SemaphoreType.DMA((4,)),
            pltpu.SemaphoreType.DMA((chunks + 2,)),
            pltpu.SemaphoreType.DMA((1,)),
            pltpu.SemaphoreType.DMA((1,)),
            pltpu.SemaphoreType.DMA((1,)),
            pltpu.SemaphoreType.DMA((n_dom,)),
        ],
        compiler_params=pltpu.CompilerParams(
            collective_id=0, has_side_effects=True
        ),
    )(
        panel_signal,
        panel_box.reshape(1, panels),
        radiation,
        reception,
        translation,
        list_source.T,
        list_class.T,
        list_count.reshape(1, boxes_all),
    )


def whole_body(n_dom, n_tm, *args):
    panel_signal, translation, boxes_all = args[0], args[4], args[5].shape[0]
    steps_own = panel_signal.shape[0]
    classes, lags, dirs_own = translation.shape
    boxes_own = boxes_all // n_dom
    fits = (
        dirs_own == LANES
        and boxes_all == LANES
        and n_dom & (n_dom - 1) == 0
        and n_tm & (n_tm - 1) == 0
        and lags == 2 * n_tm
        and steps_own * n_tm == lags
        and boxes_own == 2 * SUBLANES
        and steps_own * boxes_own == n_tm * SUBLANES
        and classes % (2 * SUBLANES) == 0
        and classes <= LANES
    )
    if fits:
        return fused_body(n_dom, n_tm, *args)
    return body(*args)


def solution(mesh):
    placed = (
        P("tm", "dom"),
        P("dom"),
        P("dom", None),
        P("dom", None),
        P(None, None, "dom"),
        P(),
        P(),
        P(),
    )
    return jax.shard_map(
        functools.partial(whole_body, mesh.shape["dom"], mesh.shape["tm"]),
        mesh=mesh, in_specs=placed, out_specs=P("tm", "dom"), check_vma=False
    )
```
